32 devices in a mesh: beams: 2 (over x), trials: 16 (over z, y, core).
Axes of the slice: x: 2, y: 2, z: 4, core: 2. Of those that a mesh axis runs over, the one named last changes fastest.
Arguments:
- spectra: bfloat16 [4096, 8192], P(('beams', 'trials')), parts along dimension 0, may hold values from -12 to 12
- delays: int32 [64, 16], P('trials'), may hold values from 0 to 56
- spans: int32 [16], replicated, may hold values from 1 to 8, as said below
- widths: int32 [8], replicated, may hold values from 1 to 128
Outputs:
- boxcar_out: float32 [128, 8, 1024], P(('beams', 'trials')), parts along dimension 0
The draws below stay inside these ranges and needn't reach their ends.
There are 2 independent parts, one for each index of `beams`. The reference program is written for one: setup_inputs(seed, part) draws one part's arguments, and reference() takes and returns one part's arrays. A program takes and returns all parts, laid end to end along the dimension named above; an argument that names none is the same for every part. Nothing has to cross between parts.
Inputs may be any that keep to these rules, and one draw needn't show every extreme that they name: Ranges come in pairs: spans[2 i] + spans[2 i + 1] = 9 for every i; some range has exactly 8 live blocks.
All inputs are finite; a program needn't handle non-finite values.
Results may differ from the reference program's by a relative error of at most 0.0003.
Values sent between devices are 32-bit elements; how exact they have to be, the bound alone decides.
No kernel may reach another device: no remote copies, remote signals or barrier semaphores. Data moves between devices by JAX's collectives and lax.ppermute only.
A program may use at most 64 MiB of HBM per device.

```python
import jax
import jax.numpy as jnp
from jax import lax

CH_SUB = 128
SAMPLE_COUNT = 8192
RANGE_TRIALS = 4
SUBT = 2
SHIFT = 8
SPAN = 8
NW = 8
KMAX = 8
NB = 64
OUT = 1024
CHANNELS = 2048
TRIALS = 64
N_TRIALS = 16


def draw_spectra(key, part):
    random_keys = jax.random.split(key, 4)
    chan = jnp.arange(CHANNELS).astype(jnp.float32)
    band = 0.5 + 1.5 * chan / CHANNELS
    common_gain = (band * jax.random.uniform(random_keys[2], (CHANNELS,), minval=0.5, maxval=2.0))[:, None]
    pulse_events = jnp.where(jax.random.uniform(random_keys[3], (1, SAMPLE_COUNT)) < 0.1, 3.0, 0.5)
    terrestrial_noise = jax.random.normal(random_keys[1], (1, SAMPLE_COUNT)) * pulse_events
    noise = jax.random.normal(random_keys[0], (CHANNELS, SAMPLE_COUNT))
    values = jnp.clip(noise + common_gain * terrestrial_noise, -12.0, 12.0)
    return values.astype(jnp.bfloat16)


def draw_spans(key, part):
    half_count = N_TRIALS // 2
    first = jax.random.randint(jax.random.fold_in(key, 11), (half_count,), 1, SPAN + 1)
    first = jnp.where(jnp.arange(half_count) == 0, SPAN, first)
    second = SPAN + 1 - first
    return jnp.stack([first, second], axis=1).reshape(N_TRIALS).astype(jnp.int32)


def plant(values, key, smallest, largest):
    spot = [jax.random.randint(jax.random.fold_in(key, axis), (), 0, length) for axis, length in enumerate(values.shape)]
    main_axis = values.shape.index(max(values.shape))
    next_to = spot[:main_axis] + [(spot[main_axis] + 1) % values.shape[main_axis]] + spot[main_axis + 1:]
    return values.at[tuple(spot)].set(smallest).at[tuple(next_to)].set(largest)


def setup_inputs(seed: int = 0, part: int = 0) -> dict:
    seeds = jax.random.split(jax.random.key(seed), 5)
    part_keys = jax.random.split(jax.random.fold_in(seeds[4], part), 5)
    spectra = draw_spectra(jax.random.fold_in(jax.random.fold_in(seeds[4], part), 71), part)
    delays = plant(jax.random.randint(seeds[1], (TRIALS, N_TRIALS), 0, NB - SPAN + 1), jax.random.fold_in(seeds[1], 1), 0, NB - SPAN).astype(jnp.int32)
    spans = draw_spans(jax.random.fold_in(seeds[4], 71), part)
    widths = plant(jax.random.randint(seeds[3], (NW,), 1, 129), jax.random.fold_in(seeds[3], 1), 1, 128).astype(jnp.int32)
    return dict(spectra=spectra, delays=delays, spans=spans, widths=widths)


def boxcars(trial, widths):
    total_len = trial.shape[1]
    prefix = jnp.cumsum(trial, axis=1)
    padded_series = jnp.concatenate([jnp.zeros_like(prefix), prefix], axis=1)

    def one_width(width):
        start = (total_len - width).astype(jnp.int32)
        lagged = lax.dynamic_slice_in_dim(padded_series, start, total_len, 1)
        return (prefix - lagged) / jnp.sqrt(width.astype(jnp.float32))
    return jax.vmap(one_width, out_axes=1)(widths)

def reference(spectra, delays, spans, widths):
    channel_mean = lax.optimization_barrier(jnp.sum(spectra.astype(jnp.float32), axis=0)) / CHANNELS
    chan = jnp.arange(CH_SUB)
    level = jnp.arange(SUBT)
    delay_in = level[:, None] * SHIFT * chan[None, :] // CH_SUB
    select = (delay_in[:, None, :] == jnp.arange(KMAX)[None, :, None]).astype(jnp.float32)
    select = select.reshape(SUBT * KMAX, CH_SUB)
    counts = lax.optimization_barrier(jnp.sum(select, axis=1))
    blocks = spectra.reshape(N_TRIALS, CH_SUB, SAMPLE_COUNT).astype(jnp.float32)
    grouped = jnp.einsum('rc,scn->srn', select, blocks)
    grouped = grouped - counts[None, :, None] * channel_mean[None, None, :]
    grouped = grouped.reshape(N_TRIALS, SUBT, KMAX, SAMPLE_COUNT)
    grouped = jnp.pad(grouped, ((0, 0), (0, 0), (0, 0), (0, KMAX)))
    time_series = grouped[:, :, 0, 0:SAMPLE_COUNT]
    for lag in range(1, KMAX):
        time_series = time_series + grouped[:, :, lag, lag:lag + SAMPLE_COUNT]
    time_series = time_series / jnp.sqrt(jnp.float32(CHANNELS))
    series_blocks = time_series.reshape(N_TRIALS, SUBT, NB, 128)
    trial_sub = (jnp.arange(TRIALS) % SUBT).astype(jnp.int32)
    offsets = jnp.arange(SPAN).astype(jnp.int32)

    def add_subband(total, subband):
        own = series_blocks[subband]
        column = delays[:, subband]
        window = own[trial_sub[:, None], column[:, None] + offsets[None, :]]
        return (total + window, None)
    start_total = jnp.zeros((TRIALS, SPAN, 128), jnp.float32)
    total, unused = lax.scan(add_subband, start_total, jnp.arange(N_TRIALS).astype(jnp.int32))
    trial = total.reshape(TRIALS, OUT)
    ranges = jnp.arange(TRIALS) // RANGE_TRIALS
    live = spans[ranges] * 128
    trial = jnp.where(jnp.arange(OUT)[None, :] < live[:, None], trial, jnp.float32(0.0))
    return boxcars(trial, widths)
```

```python
import functools

import jax
import jax.numpy as jnp
from jax import lax
from jax.experimental import pallas as pl
from jax.experimental.pallas import tpu as pltpu
from jax.sharding import PartitionSpec as P

CH_SUB = 128
SUBT = 2
SPAN = 8
KMAX = 8
LANES = 128
PER_LAG = CH_SUB // KMAX
VMEM = pltpu.MemorySpace.VMEM
SMEM = pltpu.MemorySpace.SMEM


def in_vmem(x):
    return pltpu.with_memory_space_constraint(x, VMEM)


def swap(x, bit, group):
    return lax.ppermute(x, "trials", [(i, i ^ bit) for i in range(group)])


def shifted(x, k):
    lane = lax.broadcasted_iota(jnp.int32, x.shape, 1)
    row = lax.broadcasted_iota(jnp.int32, x.shape, 0)
    here = pltpu.roll(x, LANES - k, 1)
    after = pltpu.roll(here, x.shape[0] - 1, 0)
    after = jnp.where(row == x.shape[0] - 1, 0.0, after)
    return jnp.where(lane < LANES - k, here, after)


def raw_kernel(chunks, x_hbm, out, x, sems):
    blocks = out.shape[1]
    width = x.shape[1] // chunks
    copies = []
    for i in range(chunks):
        part = pl.ds(i * width, width)
        copies.append(pltpu.make_async_copy(x_hbm.at[:, part], x.at[:, part], sems.at[i]))
        copies[-1].start()
    row = lax.broadcasted_iota(jnp.int32, (2 * KMAX, CH_SUB), 0)
    chan = lax.broadcasted_iota(jnp.int32, (2 * KMAX, CH_SUB), 1)
    select = ((row >= KMAX) | (chan // PER_LAG == KMAX - 1 - row)).astype(jnp.bfloat16)
    sub = lax.broadcasted_iota(jnp.int32, (KMAX, LANES), 0)
    lane = lax.broadcasted_iota(jnp.int32, (KMAX, LANES), 1)
    stays = lane < LANES - (KMAX - 1 - sub)
    per = width // LANES
    rolled, plain = [], []
    for i in range(chunks):
        copies[i].wait()
        sums = jnp.dot(select, x[:, i * width : (i + 1) * width], preferred_element_type=jnp.float32)
        for b in range(per):
            cut = sums[:KMAX, b * LANES : (b + 1) * LANES]
            rolled.append(pltpu.roll(cut, LANES - (KMAX - 1), 1, stride=1, stride_axis=0))
            plain.append(sums[KMAX:, b * LANES : (b + 1) * LANES])
    rolled.append(jnp.zeros((KMAX, LANES), jnp.float32))
    for b0 in range(0, blocks, 8):
        first = plain[b0]
        for k in range(1, 8):
            first = jnp.where(sub == k, plain[b0 + k], first)
        out[0, b0 : b0 + 8] = first
        level = [jnp.where(stays, rolled[b], rolled[b + 1]) for b in range(b0, b0 + 8)]
        for half in (4, 2, 1):
            low = (sub & half) == 0
            level = [
                jnp.where(low, level[k], level[k + half])
                + pltpu.roll(jnp.where(low, level[k + half], level[k]), half, 0)
                if half == 4
                else jnp.where(low, level[k] + pltpu.roll(level[k], 8 - half, 0), level[k + half] + pltpu.roll(level[k + half], half, 0))
                for k in range(half)
            ]
        out[1, b0 : b0 + 8] = level[0]


def raw_series(spectra):
    samples = spectra.shape[1]
    chunks = 4
    return pl.pallas_call(
        functools.partial(raw_kernel, chunks),
        out_shape=VMEM((SUBT, samples // LANES, LANES), jnp.float32),
        in_specs=[pl.BlockSpec(memory_space=pl.ANY)],
        out_specs=pl.BlockSpec(memory_space=VMEM),
        scratch_shapes=[pltpu.VMEM(spectra.shape, spectra.dtype), pltpu.SemaphoreType.DMA((chunks,))],
    )(spectra)


def window_kernel(masks, owners, channels, *refs):
    known = len(masks)
    raw, rest = refs[:known], refs[known:]
    delays_in, out, mean, delays, sems = rest[:owners], rest[owners], rest[owners + 1], rest[owners + 2], rest[owners + 3]
    copies = [pltpu.make_async_copy(delays_in[e], delays.at[e], sems.at[e]) for e in range(owners)]
    for c in copies:
        c.start()
    total = raw[0][0]
    for a in range(1, known):
        total = total + raw[a][0]
    mean[0] = total * (CH_SUB / channels)
    total = total * (PER_LAG / channels)
    for k in (1, 2, 4):
        total = total + shifted(total, k)
    mean[1] = total
    me = lax.axis_index("trials")
    trials, group = delays.shape[1:]
    for c in copies:
        c.wait()

    def one(e):
        for i in range(trials):
            j = i % SUBT
            acc = None
            for a in range(known):
                cut = raw[a][j, pl.ds(delays[e, i, me ^ masks[a]], SPAN), :]
                acc = cut if acc is None else acc + cut
            less = None
            if group <= 16:
                for s in range(group):
                    cut = mean[j, pl.ds(delays[e, i, s], SPAN), :]
                    less = cut if less is None else less + cut
            else:
                less = lax.fori_loop(
                    0, group, lambda s, v: v + mean[j, pl.ds(delays[e, i, s], SPAN), :], jnp.zeros_like(acc)
                )
            out[e, i] = acc - less

    if owners <= 4:
        for e in range(owners):
            one(e)
    else:
        pl.loop(0, owners)(one)


def window_sums(raw, masks, delays, channels):
    owners = len(delays)
    trials, group = delays[0].shape
    samples = raw[0].shape[1:]
    return pl.pallas_call(
        functools.partial(window_kernel, masks, owners, channels),
        out_shape=VMEM((owners, trials, SPAN, LANES), jnp.float32),
        in_specs=[pl.BlockSpec(memory_space=VMEM)] * len(raw) + [pl.BlockSpec(memory_space=pl.ANY)] * owners,
        out_specs=pl.BlockSpec(memory_space=VMEM),
        scratch_shapes=[
            pltpu.VMEM((SUBT,) + samples, jnp.float32),
            pltpu.SMEM((owners, trials, group), jnp.int32),
            pltpu.SemaphoreType.DMA((owners,)),
        ],
    )(*[in_vmem(r) for r in raw], *delays)


def boxcar_kernel(channels, parts, *refs):
    ins, (spans_in, widths_in, out, spans, widths, sems) = refs[:parts], refs[parts:]
    copies = [
        pltpu.make_async_copy(spans_in, spans, sems.at[0]),
        pltpu.make_async_copy(widths_in, widths, sems.at[1]),
    ]
    for c in copies:
        c.start()
    trial = ins[0][...]
    for p in range(1, parts):
        trial = trial + ins[p][...]
    trials = trial.shape[0]
    flat = trial.reshape(trials * SPAN, LANES)
    block = lax.broadcasted_iota(jnp.int32, flat.shape, 0) % SPAN
    lane = lax.broadcasted_iota(jnp.int32, flat.shape, 1)
    copies[0].wait()
    flat = jnp.where(block < spans[lax.axis_index("trials")], flat, 0.0)
    prefix = flat
    for k in (1, 2, 4, 8, 16, 32, 64):
        prefix = prefix + jnp.where(lane >= k, pltpu.roll(prefix, k, 1), 0.0)
    ends = jnp.broadcast_to(prefix[:, LANES - 1 :], prefix.shape)
    before = jnp.where(block >= 1, pltpu.roll(ends, 1, 0), 0.0)
    for k in (1, 2, 4):
        before = before + jnp.where(block >= k, pltpu.roll(before, k, 0), 0.0)
    prefix = prefix + before
    copies[1].wait()
    for w in range(widths.shape[0]):
        width = widths[w]
        scale = 1.0 / (jnp.sqrt(jnp.full((SPAN, LANES), width, jnp.float32)) * (channels**0.5))
        here = pltpu.roll(prefix, width, 1)
        last = jnp.where(block >= 1, pltpu.roll(here, 1, 0), 0.0)
        lagged = jnp.where(lane >= width, here, last)
        diff = (prefix - lagged).reshape(trials, SPAN, LANES)
        for t in range(trials):
            out[t, :, w, :] = diff[t] * scale


def boxcars(parts, spans, widths, channels):
    trials = parts[0].shape[0]
    nw = widths.shape[0]
    out = pl.pallas_call(
        functools.partial(boxcar_kernel, channels, len(parts)),
        out_shape=jax.ShapeDtypeStruct((trials, SPAN, nw, LANES), jnp.float32),
        in_specs=[pl.BlockSpec(memory_space=VMEM)] * len(parts) + [pl.BlockSpec(memory_space=pl.ANY)] * 2,
        out_specs=pl.BlockSpec(memory_space=VMEM),
        scratch_shapes=[
            pltpu.SMEM(spans.shape, jnp.int32),
            pltpu.SMEM(widths.shape, jnp.int32),
            pltpu.SemaphoreType.DMA((2,)),
        ],
    )(*[in_vmem(p) for p in parts], spans, widths)
    return out.transpose(0, 2, 1, 3).reshape(trials, nw, SPAN * LANES)


def on_device(spectra, delays, spans, widths):
    group = lax.axis_size("trials")
    channels = CH_SUB * group
    gather_bits = [b for b in (2, 4) if b < group]
    sum_bits = [b for b in (1, 8, 16, 32, 64, 128, 256) if b < group]

    raw = [raw_series(spectra)]
    masks = [0]
    for b in gather_bits:
        raw = raw + [swap(r, b, group) for r in raw]
        masks = masks + [m ^ b for m in masks]

    owned = [delays]
    for b in reversed(sum_bits):
        owned = owned + [swap(d, b, group) for d in owned]

    sums = window_sums(raw, masks, owned, channels)
    for n, b in enumerate(sum_bits):
        half = sums.shape[0] // 2
        mine, theirs = sums[:half], swap(sums[half:], b, group)
        if n + 1 < len(sum_bits):
            sums = mine + theirs
    return boxcars([mine[0], theirs[0]], spans, widths, channels)


def solution(mesh):
    in_specs = (P(("beams", "trials"), None), P("trials", None), P(), P())
    out_specs = P(("beams", "trials"), None, None)
    return jax.shard_map(
        on_device, mesh=mesh, in_specs=in_specs, out_specs=out_specs, check_vma=False
    )
```

```python
import functools

import jax
import jax.numpy as jnp
from jax import lax
from jax.experimental import pallas as pl
from jax.experimental.pallas import tpu as pltpu
from jax.sharding import PartitionSpec as P

CH_SUB = 128
SUBT = 2
SPAN = 8
KMAX = 8
LANES = 128
PER_LAG = CH_SUB // KMAX
VMEM = pltpu.MemorySpace.VMEM
SMEM = pltpu.MemorySpace.SMEM
IN_VMEM = pl.BlockSpec(memory_space=VMEM)
IN_SMEM = pl.BlockSpec(memory_space=SMEM)


def in_vmem(x):
    return pltpu.with_memory_space_constraint(x, VMEM)


def in_smem(x):
    return pltpu.with_memory_space_constraint(x, SMEM)


def cost(flops, read):
    return pl.CostEstimate(flops=flops, bytes_accessed=read, transcendentals=0)


def swap(x, bit, group):
    return lax.ppermute(x, "trials", [(i, i ^ bit) for i in range(group)])


def shifted(x, k):
    lane = lax.broadcasted_iota(jnp.int32, x.shape, 1)
    row = lax.broadcasted_iota(jnp.int32, x.shape, 0)
    here = pltpu.roll(x, LANES - k, 1)
    after = pltpu.roll(here, x.shape[0] - 1, 0)
    after = jnp.where(row == x.shape[0] - 1, 0.0, after)
    return jnp.where(lane < LANES - k, here, after)


def raw_kernel(chunks, x_hbm, delays_hbm, out, rows, x, delays, sems):
    blocks = x.shape[1] // LANES
    width = x.shape[1] // chunks
    copies = []
    for i in range(chunks):
        part = pl.ds(i * width, width)
        copies.append(pltpu.make_async_copy(x_hbm.at[:, part], x.at[:, part], sems.at[i]))
        copies[-1].start()
    copies.append(pltpu.make_async_copy(delays_hbm, delays, sems.at[chunks]))
    copies[-1].start()
    row = lax.broadcasted_iota(jnp.int32, (2 * KMAX, CH_SUB), 0)
    chan = lax.broadcasted_iota(jnp.int32, (2 * KMAX, CH_SUB), 1)
    select = ((row >= KMAX) | (chan // PER_LAG == KMAX - 1 - row)).astype(jnp.bfloat16)
    sub = lax.broadcasted_iota(jnp.int32, (KMAX, LANES), 0)
    lane = lax.broadcasted_iota(jnp.int32, (KMAX, LANES), 1)
    stays = lane < LANES - (KMAX - 1 - sub)
    rows[...] = jnp.zeros_like(rows)
    rolled, plain = [], []

    def finish(b0):
        first = plain[b0]
        for k in range(1, 8):
            first = jnp.where(sub == k, plain[b0 + k], first)
        out[0, b0 : b0 + 8] = first
        level = [jnp.where(stays, rolled[b], rolled[b + 1]) for b in range(b0, b0 + 8)]
        for half in (4, 2, 1):
            low = (sub & half) == 0
            level = [
                jnp.where(low, level[k] + pltpu.roll(level[k], 8 - half, 0), level[k + half] + pltpu.roll(level[k + half], half, 0))
                for k in range(half)
            ]
        out[1, b0 : b0 + 8] = level[0]

    for b0 in range(0, blocks, 8):
        if b0 * LANES % width == 0:
            copies[b0 * LANES // width].wait()
        part = x[:, b0 * LANES : (b0 + 8) * LANES]
        sums = jnp.dot(select, part, preferred_element_type=jnp.float32)
        for b in range(8):
            cut = sums[:KMAX, b * LANES : (b + 1) * LANES]
            rolled.append(pltpu.roll(cut, LANES - (KMAX - 1), 1, stride=1, stride_axis=0))
            plain.append(sums[KMAX:, b * LANES : (b + 1) * LANES])
        if b0:
            finish(b0 - 8)
    rolled.append(jnp.zeros((KMAX, LANES), jnp.float32))
    finish(blocks - 8)
    copies[chunks].wait()
    rows[: delays.shape[0], : delays.shape[1]] = delays[...]


def raw_series(spectra, delays):
    channels, samples = spectra.shape
    chunks = 2
    return pl.pallas_call(
        functools.partial(raw_kernel, chunks),
        out_shape=(VMEM((SUBT, samples // LANES, LANES), jnp.float32), VMEM((8, LANES), jnp.int32)),
        in_specs=[pl.BlockSpec(memory_space=pl.ANY)] * 2,
        out_specs=(IN_VMEM,) * 2,
        scratch_shapes=[
            pltpu.VMEM(spectra.shape, spectra.dtype),
            pltpu.VMEM(delays.shape, delays.dtype),
            pltpu.SemaphoreType.DMA((chunks + 1,)),
        ],
        cost_estimate=cost(4 * KMAX * channels * samples, 2 * channels * samples),
    )(spectra, delays)


def pack_kernel(mine, theirs, both):
    core = lax.axis_index("trials") & 1
    first = core == 0
    both[...] = jnp.zeros_like(both)
    rows, cols = theirs.shape
    both[0, :rows, :cols] = jnp.where(first, mine[:rows, :cols], theirs[...])
    both[1, :rows, :cols] = jnp.where(first, theirs[...], mine[:rows, :cols])


def pack_delays(mine, theirs):
    return pl.pallas_call(
        pack_kernel,
        out_shape=VMEM((2,) + mine.shape, jnp.int32),
        in_specs=[IN_VMEM] * 2,
        out_specs=IN_VMEM,
        cost_estimate=cost(0, 1 << 20),
    )(in_vmem(mine), in_vmem(theirs))


def scalars_kernel(x, out, sem):
    copy = pltpu.make_async_copy(x, out, sem)
    copy.start()
    copy.wait()


def to_scalars(x):
    return pl.pallas_call(
        scalars_kernel,
        out_shape=SMEM(x.shape, x.dtype),
        in_specs=[IN_VMEM],
        out_specs=IN_SMEM,
        scratch_shapes=[pltpu.SemaphoreType.DMA(())],
        cost_estimate=cost(0, 1 << 20),
    )(in_vmem(x))


def tables_kernel(channels, widths, spans, bands, scale, mask):
    lag = lax.broadcasted_iota(jnp.int32, (LANES, LANES), 1) - lax.broadcasted_iota(jnp.int32, (LANES, LANES), 0)
    row = lax.broadcasted_iota(jnp.int32, (SPAN, LANES), 0)
    for n in range(widths.shape[0]):
        width = widths[n]
        cols = pl.ds(n * LANES, LANES)
        bands[:LANES, cols] = ((lag >= 0) & (lag < width)).astype(jnp.bfloat16)
        bands[LANES:, cols] = (lag + LANES < width).astype(jnp.bfloat16)
        scale[n : n + 1] = 1.0 / (jnp.sqrt(jnp.full((1, LANES), width, jnp.float32)) * (channels**0.5))
    mask[...] = (row < spans[lax.axis_index("trials")]).astype(jnp.float32)


def tables(widths, spans, channels):
    nw = widths.shape[0]
    return pl.pallas_call(
        functools.partial(tables_kernel, channels),
        out_shape=(
            VMEM((2 * LANES, nw * LANES), jnp.bfloat16),
            VMEM((nw, LANES), jnp.float32),
            VMEM((SPAN, LANES), jnp.float32),
        ),
        in_specs=[IN_SMEM] * 2,
        out_specs=(IN_VMEM,) * 3,
        cost_estimate=cost(0, 1 << 20),
    )(widths, spans)


def windows(out, e, raw, masks, mean, delays, row, trials, group):
    me = lax.axis_index("trials")
    for i in range(trials):
        j = i % SUBT
        acc = None
        for a, ref in enumerate(raw):
            cut = ref[j, pl.ds(delays[row, i, me ^ masks[a]], SPAN), :]
            acc = cut if acc is None else acc + cut
        less = None
        if group <= 16:
            for s in range(group):
                cut = mean[j, pl.ds(delays[row, i, s], SPAN), :]
                less = cut if less is None else less + cut
        else:
            less = lax.fori_loop(
                0, group, lambda s, v: v + mean[j, pl.ds(delays[row, i, s], SPAN), :], jnp.zeros_like(acc)
            )
        out[e, i] = acc - less


def near_kernel(masks, trials, group, channels, *refs):
    known = len(masks)
    raw, (near, keep, send, mean) = refs[:known], refs[known:]
    total = raw[0][0]
    for a in range(1, known):
        total = total + raw[a][0]
    mean[0] = total * (CH_SUB / channels)
    total = total * (PER_LAG / channels)
    for k in (1, 2, 4):
        total = total + shifted(total, k)
    mean[1] = total
    core = lax.axis_index("trials") & 1
    windows(keep, 0, raw, masks, mean, near, core, trials, group)
    windows(send, 0, raw, masks, mean, near, 1 - core, trials, group)


def near_sums(raw, masks, near, trials, group):
    one = VMEM((1, trials, SPAN, LANES), jnp.float32)
    return pl.pallas_call(
        functools.partial(near_kernel, masks, trials, group, CH_SUB * group),
        out_shape=(one, one, VMEM(raw[0].shape, jnp.float32)),
        in_specs=[IN_VMEM] * len(raw) + [IN_SMEM],
        out_specs=(IN_VMEM,) * 3,
        cost_estimate=cost(0, 1 << 20),
    )(*[in_vmem(r) for r in raw], in_smem(near))


def far_kernel(masks, trials, group, *refs):
    known = len(masks)
    raw, (mean, keep_near, send_near, far_in, keep, send, far, sem) = refs[:known], refs[known:]
    copy = pltpu.make_async_copy(far_in, far, sem)
    copy.start()
    core = lax.axis_index("trials") & 1
    chips = far.shape[0] // 2
    keep[:1] = keep_near[...]
    send[:1] = send_near[...]
    copy.wait()

    def chip(e):
        windows(send, e + 1, raw, masks, mean, far, 2 * e + 1 - core, trials, group)
        windows(keep, e + 1, raw, masks, mean, far, 2 * e + core, trials, group)

    if chips == 1:
        chip(0)
    else:
        pl.loop(0, chips)(chip)


def far_sums(raw, masks, mean, keep, send, far, group):
    trials = keep.shape[1]
    half = VMEM((far.shape[0] // 2 + 1, trials, SPAN, LANES), jnp.float32)
    return pl.pallas_call(
        functools.partial(far_kernel, masks, trials, group),
        out_shape=(half, half),
        in_specs=[IN_VMEM] * (len(raw) + 4),
        out_specs=(IN_VMEM,) * 2,
        scratch_shapes=[pltpu.SMEM(far.shape, jnp.int32), pltpu.SemaphoreType.DMA(())],
        cost_estimate=cost(0, 1 << 20),
    )(*[in_vmem(v) for v in (*raw, mean, keep, send, far)])


def boxcar_kernel(a, b, bands, scale, mask, out, y, sems):
    trials = a.shape[0]
    rows = trials * SPAN
    trial = jnp.where(mask[...][None] > 0.0, a[...] + b[...], 0.0).reshape(rows, LANES)
    block = lax.broadcasted_iota(jnp.int32, trial.shape, 0) % SPAN
    before = jnp.where(block >= 1, pltpu.roll(trial, 1, 0), 0.0)
    rest = jnp.concatenate([trial, before], axis=1)
    pieces = []
    for _ in range(3):
        pieces.append(rest.astype(jnp.bfloat16))
        rest = rest - pieces[-1].astype(jnp.float32)
    sums = jnp.dot(jnp.concatenate(pieces, axis=0), bands[...], preferred_element_type=jnp.float32)
    sums = sums[:rows] + (sums[rows : 2 * rows] + sums[2 * rows :])
    copies = []
    for t in range(trials):
        for n in range(scale.shape[0]):
            y[t, :, n, :] = sums[t * SPAN : (t + 1) * SPAN, n * LANES : (n + 1) * LANES] * scale[n : n + 1]
        copies.append(pltpu.make_async_copy(y.at[t], out.at[t], sems.at[t]))
        copies[-1].start()
    for c in copies:
        c.wait()


def boxcars(a, b, bands, scale, mask):
    trials, nw = a.shape[0], scale.shape[0]
    shape = (trials, SPAN, nw, LANES)
    out = pl.pallas_call(
        boxcar_kernel,
        out_shape=jax.ShapeDtypeStruct(shape, jnp.float32),
        in_specs=[IN_VMEM] * 5,
        out_specs=pl.BlockSpec(memory_space=pl.ANY),
        scratch_shapes=[pltpu.VMEM(shape, jnp.float32), pltpu.SemaphoreType.DMA((trials,))],
        cost_estimate=cost(0, 1 << 20),
    )(*[in_vmem(v) for v in (a, b, bands, scale, mask)])
    return out.transpose(0, 2, 1, 3).reshape(trials, nw, SPAN * LANES)


def on_device(spectra, delays, spans, widths):
    group = lax.axis_size("trials")
    channels = CH_SUB * group
    trials = delays.shape[0]
    masks = (0, 2, 4, 6)
    far_bits = [b for b in (8, 16, 32, 64, 128, 256) if b < group]

    raw, rows = raw_series(spectra, delays)
    raws = [raw] + [swap(raw, m, group) for m in masks[1:]]
    owned = pack_delays(rows, swap(delays, 1, group))
    near = to_scalars(owned)
    for b in far_bits:
        owned = jnp.concatenate([owned, swap(owned, b, group)])[2 if b == far_bits[-1] else 0 :]
    boxes = tables(widths, spans, channels)

    keep, send, mean = near_sums(raws, masks, near, trials, group)
    keep, send = far_sums(raws, masks, mean, keep, send, owned, group)
    theirs = swap(send, 1, group)
    for b in reversed(far_bits):
        sums = keep + theirs
        half = sums.shape[0] // 2
        keep, theirs = sums[:half], swap(sums[half:], b, group)
    return boxcars(keep[0], theirs[0], *boxes)


def solution(mesh):
    in_specs = (P(("beams", "trials"), None), P("trials", None), P(), P())
    out_specs = P(("beams", "trials"), None, None)
    return jax.shard_map(
        on_device, mesh=mesh, in_specs=in_specs, out_specs=out_specs, check_vma=False
    )
```

```python
import functools

import jax
import jax.numpy as jnp
from jax import lax
from jax.experimental import pallas as pl
from jax.experimental.pallas import tpu as pltpu
from jax.sharding import PartitionSpec as P

CH_SUB = 128
SUBT = 2
SPAN = 8
KMAX = 8
LANES = 128
PER_LAG = CH_SUB // KMAX
VMEM = pltpu.MemorySpace.VMEM
SMEM = pltpu.MemorySpace.SMEM
IN_VMEM = pl.BlockSpec(memory_space=VMEM)
IN_SMEM = pl.BlockSpec(memory_space=SMEM)


def in_vmem(x):
    return pltpu.with_memory_space_constraint(x, VMEM)


def in_smem(x):
    return pltpu.with_memory_space_constraint(x, SMEM)


def cost(flops, read):
    return pl.CostEstimate(flops=flops, bytes_accessed=read, transcendentals=0)


def swap(x, bit, group):
    return lax.ppermute(x, "trials", [(i, i ^ bit) for i in range(group)])


def shifted(x, k):
    lane = lax.broadcasted_iota(jnp.int32, x.shape, 1)
    row = lax.broadcasted_iota(jnp.int32, x.shape, 0)
    here = pltpu.roll(x, LANES - k, 1)
    after = pltpu.roll(here, x.shape[0] - 1, 0)
    after = jnp.where(row == x.shape[0] - 1, 0.0, after)
    return jnp.where(lane < LANES - k, here, after)


def raw_kernel(chunks, x_hbm, delays_hbm, out, rows, x, delays, sems):
    blocks = x.shape[1] // LANES
    width = x.shape[1] // chunks
    copies = []
    for i in range(chunks):
        part = pl.ds(i * width, width)
        copies.append(pltpu.make_async_copy(x_hbm.at[:, part], x.at[:, part], sems.at[i]))
        copies[-1].start()
    copies.append(pltpu.make_async_copy(delays_hbm, delays, sems.at[chunks]))
    copies[-1].start()
    row = lax.broadcasted_iota(jnp.int32, (2 * KMAX, CH_SUB), 0)
    chan = lax.broadcasted_iota(jnp.int32, (2 * KMAX, CH_SUB), 1)
    select = ((row >= KMAX) | (chan // PER_LAG == KMAX - 1 - row)).astype(jnp.bfloat16)
    sub = lax.broadcasted_iota(jnp.int32, (KMAX, LANES), 0)
    lane = lax.broadcasted_iota(jnp.int32, (KMAX, LANES), 1)
    stays = lane < LANES - (KMAX - 1 - sub)
    rows[...] = jnp.zeros_like(rows)
    rolled, plain = [], []

    def finish(b0):
        first = plain[b0]
        for k in range(1, 8):
            first = jnp.where(sub == k, plain[b0 + k], first)
        out[0, b0 : b0 + 8] = first
        level = [jnp.where(stays, rolled[b], rolled[b + 1]) for b in range(b0, b0 + 8)]
        for half in (4, 2, 1):
            low = (sub & half) == 0
            level = [
                jnp.where(low, level[k] + pltpu.roll(level[k], 8 - half, 0), level[k + half] + pltpu.roll(level[k + half], half, 0))
                for k in range(half)
            ]
        out[1, b0 : b0 + 8] = level[0]

    for b0 in range(0, blocks, 8):
        if b0 * LANES % width == 0:
            copies[b0 * LANES // width].wait()
        part = x[:, b0 * LANES : (b0 + 8) * LANES]
        sums = jnp.dot(select, part, preferred_element_type=jnp.float32)
        for b in range(8):
            cut = sums[:KMAX, b * LANES : (b + 1) * LANES]
            rolled.append(pltpu.roll(cut, LANES - (KMAX - 1), 1, stride=1, stride_axis=0))
            plain.append(sums[KMAX:, b * LANES : (b + 1) * LANES])
        if b0:
            finish(b0 - 8)
    rolled.append(jnp.zeros((KMAX, LANES), jnp.float32))
    finish(blocks - 8)
    copies[chunks].wait()
    rows[: delays.shape[0], : delays.shape[1]] = delays[...]


def raw_series(spectra, delays):
    channels, samples = spectra.shape
    chunks = 2
    return pl.pallas_call(
        functools.partial(raw_kernel, chunks),
        out_shape=(VMEM((SUBT, samples // LANES, LANES), jnp.float32), VMEM((8, LANES), jnp.int32)),
        in_specs=[pl.BlockSpec(memory_space=pl.ANY)] * 2,
        out_specs=(IN_VMEM,) * 2,
        scratch_shapes=[
            pltpu.VMEM(spectra.shape, spectra.dtype),
            pltpu.VMEM(delays.shape, delays.dtype),
            pltpu.SemaphoreType.DMA((chunks + 1,)),
        ],
        cost_estimate=cost(4 * KMAX * channels * samples, 2 * channels * samples),
    )(spectra, delays)


def pack_kernel(mine, theirs, both):
    core = lax.axis_index("trials") & 1
    first = core == 0
    both[...] = jnp.zeros_like(both)
    rows, cols = theirs.shape
    both[0, :rows, :cols] = jnp.where(first, mine[:rows, :cols], theirs[...])
    both[1, :rows, :cols] = jnp.where(first, theirs[...], mine[:rows, :cols])


def pack_delays(mine, theirs):
    return pl.pallas_call(
        pack_kernel,
        out_shape=VMEM((2,) + mine.shape, jnp.int32),
        in_specs=[IN_VMEM] * 2,
        out_specs=IN_VMEM,
        cost_estimate=cost(0, 1 << 20),
    )(in_vmem(mine), in_vmem(theirs))


def scalars_kernel(x, out, sem):
    copy = pltpu.make_async_copy(x, out, sem)
    copy.start()
    copy.wait()


def to_scalars(x):
    return pl.pallas_call(
        scalars_kernel,
        out_shape=SMEM(x.shape, x.dtype),
        in_specs=[IN_VMEM],
        out_specs=IN_SMEM,
        scratch_shapes=[pltpu.SemaphoreType.DMA(())],
        cost_estimate=cost(0, 1 << 20),
    )(in_vmem(x))


def tables_kernel(channels, widths, spans, bands, scale, mask):
    lag = lax.broadcasted_iota(jnp.int32, (LANES, LANES), 1) - lax.broadcasted_iota(jnp.int32, (LANES, LANES), 0)
    row = lax.broadcasted_iota(jnp.int32, (SPAN, LANES), 0)
    for n in range(widths.shape[0]):
        width = widths[n]
        cols = pl.ds(n * LANES, LANES)
        bands[:LANES, cols] = ((lag >= 0) & (lag < width)).astype(jnp.bfloat16)
        bands[LANES:, cols] = (lag + LANES < width).astype(jnp.bfloat16)
        scale[n : n + 1] = 1.0 / (jnp.sqrt(jnp.full((1, LANES), width, jnp.float32)) * (channels**0.5))
    mask[...] = (row < spans[lax.axis_index("trials")]).astype(jnp.float32)


def tables(widths, spans, channels):
    nw = widths.shape[0]
    return pl.pallas_call(
        functools.partial(tables_kernel, channels),
        out_shape=(
            VMEM((2 * LANES, nw * LANES), jnp.bfloat16),
            VMEM((nw, LANES), jnp.float32),
            VMEM((SPAN, LANES), jnp.float32),
        ),
        in_specs=[IN_SMEM] * 2,
        out_specs=(IN_VMEM,) * 3,
        cost_estimate=cost(0, 1 << 20),
    )(widths, spans)


def windows(out, e, raw, masks, mean, delays, row, trials, group):
    me = lax.axis_index("trials")
    for i in range(trials):
        j = i % SUBT
        acc = None
        for a, ref in enumerate(raw):
            cut = ref[j, pl.ds(delays[row, i, me ^ masks[a]], SPAN), :]
            acc = cut if acc is None else acc + cut
        less = None
        if group <= 16:
            for s in range(group):
                cut = mean[j, pl.ds(delays[row, i, s], SPAN), :]
                less = cut if less is None else less + cut
        else:
            less = lax.fori_loop(
                0, group, lambda s, v: v + mean[j, pl.ds(delays[row, i, s], SPAN), :], jnp.zeros_like(acc)
            )
        out[e, i] = acc - less


def near_kernel(masks, trials, group, channels, *refs):
    known = len(masks)
    raw, (near, keep, send, mean) = refs[:known], refs[known:]
    total = raw[0][0]
    for a in range(1, known):
        total = total + raw[a][0]
    mean[0] = total * (CH_SUB / channels)
    total = total * (PER_LAG / channels)
    for k in (1, 2, 4):
        total = total + shifted(total, k)
    mean[1] = total
    core = lax.axis_index("trials") & 1
    windows(keep, 0, raw, masks, mean, near, core, trials, group)
    windows(send, 0, raw, masks, mean, near, 1 - core, trials, group)


def near_sums(raw, masks, near, trials, group):
    one = VMEM((1, trials, SPAN, LANES), jnp.float32)
    return pl.pallas_call(
        functools.partial(near_kernel, masks, trials, group, CH_SUB * group),
        out_shape=(one, one, VMEM(raw[0].shape, jnp.float32)),
        in_specs=[IN_VMEM] * len(raw) + [IN_SMEM],
        out_specs=(IN_VMEM,) * 3,
        cost_estimate=cost(0, 1 << 20),
    )(*[in_vmem(r) for r in raw], in_smem(near))


def far_kernel(masks, trials, group, *refs):
    known = len(masks)
    raw, (mean, keep_near, send_near, far_in, keep, send, far, sem) = refs[:known], refs[known:]
    core = lax.axis_index("trials") & 1
    chips = far.shape[0] // 2
    if chips == 1:
        for row in range(2):
            tile = far_in[row]
            for i in range(trials):
                for s in range(group):
                    far[row, i, s] = tile[i, s]
    else:
        copy = pltpu.make_async_copy(far_in, far, sem)
        copy.start()
        copy.wait()
    keep[:1] = keep_near[...]
    send[:1] = send_near[...]

    def chip(e):
        windows(send, e + 1, raw, masks, mean, far, 2 * e + 1 - core, trials, group)
        windows(keep, e + 1, raw, masks, mean, far, 2 * e + core, trials, group)

    if chips == 1:
        chip(0)
    else:
        pl.loop(0, chips)(chip)


def far_sums(raw, masks, mean, keep, send, far, group):
    trials = keep.shape[1]
    half = VMEM((far.shape[0] // 2 + 1, trials, SPAN, LANES), jnp.float32)
    return pl.pallas_call(
        functools.partial(far_kernel, masks, trials, group),
        out_shape=(half, half),
        in_specs=[IN_VMEM] * (len(raw) + 4),
        out_specs=(IN_VMEM,) * 2,
        scratch_shapes=[pltpu.SMEM(far.shape, jnp.int32), pltpu.SemaphoreType.DMA(())],
        cost_estimate=cost(0, 1 << 20),
    )(*[in_vmem(v) for v in (*raw, mean, keep, send, far)])


def boxcar_kernel(a, b, bands, scale, mask, out, y, sems):
    trials = a.shape[0]
    rows = trials * SPAN
    trial = jnp.where(mask[...][None] > 0.0, a[...] + b[...], 0.0).reshape(rows, LANES)
    block = lax.broadcasted_iota(jnp.int32, trial.shape, 0) % SPAN
    before = jnp.where(block >= 1, pltpu.roll(trial, 1, 0), 0.0)
    rest = jnp.concatenate([trial, before], axis=1)
    pieces = []
    for _ in range(3):
        pieces.append(rest.astype(jnp.bfloat16))
        rest = rest - pieces[-1].astype(jnp.float32)
    sums = jnp.dot(jnp.concatenate(pieces, axis=0), bands[...], preferred_element_type=jnp.float32)
    sums = sums[:rows] + (sums[rows : 2 * rows] + sums[2 * rows :])
    copies = []
    for t in range(trials):
        for n in range(scale.shape[0]):
            y[t, :, n, :] = sums[t * SPAN : (t + 1) * SPAN, n * LANES : (n + 1) * LANES] * scale[n : n + 1]
        copies.append(pltpu.make_async_copy(y.at[t], out.at[t], sems.at[t]))
        copies[-1].start()
    for c in copies:
        c.wait()


def boxcars(a, b, bands, scale, mask):
    trials, nw = a.shape[0], scale.shape[0]
    shape = (trials, SPAN, nw, LANES)
    out = pl.pallas_call(
        boxcar_kernel,
        out_shape=jax.ShapeDtypeStruct(shape, jnp.float32),
        in_specs=[IN_VMEM] * 5,
        out_specs=pl.BlockSpec(memory_space=pl.ANY),
        scratch_shapes=[pltpu.VMEM(shape, jnp.float32), pltpu.SemaphoreType.DMA((trials,))],
        cost_estimate=cost(0, 1 << 20),
    )(*[in_vmem(v) for v in (a, b, bands, scale, mask)])
    return out.transpose(0, 2, 1, 3).reshape(trials, nw, SPAN * LANES)


def on_device(spectra, delays, spans, widths):
    group = lax.axis_size("trials")
    channels = CH_SUB * group
    trials = delays.shape[0]
    masks = (0, 2, 4, 6)
    far_bits = [b for b in (8, 16, 32, 64, 128, 256) if b < group]

    raw, rows = raw_series(spectra, delays)
    raw, theirs = lax.optimization_barrier((raw, swap(delays, 1, group)))
    raws = [raw] + [swap(raw, m, group) for m in masks[1:]]
    owned = pack_delays(rows, theirs)
    near = to_scalars(owned)
    for b in far_bits:
        owned = jnp.concatenate([owned, swap(owned, b, group)])[2 if b == far_bits[-1] else 0 :]
    boxes = tables(widths, spans, channels)

    keep, send, mean = near_sums(raws, masks, near, trials, group)
    keep, send = far_sums(raws, masks, mean, keep, send, owned, group)
    theirs = swap(send, 1, group)
    for b in reversed(far_bits):
        sums = keep + theirs
        half = sums.shape[0] // 2
        keep, theirs = sums[:half], swap(sums[half:], b, group)
    return boxcars(keep[0], theirs[0], *boxes)


def solution(mesh):
    in_specs = (P(("beams", "trials"), None), P("trials", None), P(), P())
    out_specs = P(("beams", "trials"), None, None)
    return jax.shard_map(
        on_device, mesh=mesh, in_specs=in_specs, out_specs=out_specs, check_vma=False
    )
```

```python
import functools

import jax
import jax.numpy as jnp
from jax import lax
from jax.experimental import pallas as pl
from jax.experimental.pallas import tpu as pltpu
from jax.sharding import PartitionSpec as P

CH_SUB = 128
SUBT = 2
SPAN = 8
KMAX = 8
LANES = 128
PER_LAG = CH_SUB // KMAX
VMEM = pltpu.MemorySpace.VMEM
SMEM = pltpu.MemorySpace.SMEM
IN_VMEM = pl.BlockSpec(memory_space=VMEM)
IN_SMEM = pl.BlockSpec(memory_space=SMEM)


def in_vmem(x):
    return pltpu.with_memory_space_constraint(x, VMEM)


def in_smem(x):
    return pltpu.with_memory_space_constraint(x, SMEM)


def cost(flops, read):
    return pl.CostEstimate(flops=flops, bytes_accessed=read, transcendentals=0)


def swap(x, bit, group):
    return lax.ppermute(x, "trials", [(i, i ^ bit) for i in range(group)])


def shifted(x, k):
    lane = lax.broadcasted_iota(jnp.int32, x.shape, 1)
    row = lax.broadcasted_iota(jnp.int32, x.shape, 0)
    here = pltpu.roll(x, LANES - k, 1)
    after = pltpu.roll(here, x.shape[0] - 1, 0)
    after = jnp.where(row == x.shape[0] - 1, 0.0, after)
    return jnp.where(lane < LANES - k, here, after)


def raw_kernel(chunks, x_hbm, delays_hbm, out, rows, x, delays, sems):
    blocks = x.shape[1] // LANES
    width = x.shape[1] // chunks
    copies = []
    for i in range(chunks):
        part = pl.ds(i * width, width)
        copies.append(pltpu.make_async_copy(x_hbm.at[:, part], x.at[:, part], sems.at[i]))
        copies[-1].start()
    copies.append(pltpu.make_async_copy(delays_hbm, delays, sems.at[chunks]))
    copies[-1].start()
    row = lax.broadcasted_iota(jnp.int32, (2 * KMAX, CH_SUB), 0)
    chan = lax.broadcasted_iota(jnp.int32, (2 * KMAX, CH_SUB), 1)
    select = ((row >= KMAX) | (chan // PER_LAG == KMAX - 1 - row)).astype(jnp.bfloat16)
    sub = lax.broadcasted_iota(jnp.int32, (KMAX, LANES), 0)
    lane = lax.broadcasted_iota(jnp.int32, (KMAX, LANES), 1)
    stays = lane < LANES - (KMAX - 1 - sub)
    rows[...] = jnp.zeros_like(rows)
    rolled, plain = [], []

    def finish(b0):
        first = plain[b0]
        for k in range(1, 8):
            first = jnp.where(sub == k, plain[b0 + k], first)
        out[0, b0 : b0 + 8] = first
        level = [jnp.where(stays, rolled[b], rolled[b + 1]) for b in range(b0, b0 + 8)]
        for half in (4, 2, 1):
            low = (sub & half) == 0
            level = [
                jnp.where(low, level[k] + pltpu.roll(level[k], 8 - half, 0), level[k + half] + pltpu.roll(level[k + half], half, 0))
                for k in range(half)
            ]
        out[1, b0 : b0 + 8] = level[0]

    for b0 in range(0, blocks, 8):
        if b0 * LANES % width == 0:
            copies[b0 * LANES // width].wait()
        part = x[:, b0 * LANES : (b0 + 8) * LANES]
        sums = jnp.dot(select, part, preferred_element_type=jnp.float32)
        for b in range(8):
            cut = sums[:KMAX, b * LANES : (b + 1) * LANES]
            rolled.append(pltpu.roll(cut, LANES - (KMAX - 1), 1, stride=1, stride_axis=0))
            plain.append(sums[KMAX:, b * LANES : (b + 1) * LANES])
        if b0:
            finish(b0 - 8)
    rolled.append(jnp.zeros((KMAX, LANES), jnp.float32))
    finish(blocks - 8)
    copies[chunks].wait()
    rows[: delays.shape[0], : delays.shape[1]] = delays[...]


def raw_series(spectra, delays):
    channels, samples = spectra.shape
    chunks = 2
    return pl.pallas_call(
        functools.partial(raw_kernel, chunks),
        out_shape=(VMEM((SUBT, samples // LANES, LANES), jnp.float32), VMEM((8, LANES), jnp.int32)),
        in_specs=[pl.BlockSpec(memory_space=pl.ANY)] * 2,
        out_specs=(IN_VMEM,) * 2,
        scratch_shapes=[
            pltpu.VMEM(spectra.shape, spectra.dtype),
            pltpu.VMEM(delays.shape, delays.dtype),
            pltpu.SemaphoreType.DMA((chunks + 1,)),
        ],
        cost_estimate=cost(4 * KMAX * channels * samples, 2 * channels * samples),
    )(spectra, delays)


def pack_kernel(mine, theirs, both):
    core = lax.axis_index("trials") & 1
    first = core == 0
    both[...] = jnp.zeros_like(both)
    rows, cols = theirs.shape
    both[0, :rows, :cols] = jnp.where(first, mine[:rows, :cols], theirs[...])
    both[1, :rows, :cols] = jnp.where(first, theirs[...], mine[:rows, :cols])


def pack_delays(mine, theirs):
    return pl.pallas_call(
        pack_kernel,
        out_shape=VMEM((2,) + mine.shape, jnp.int32),
        in_specs=[IN_VMEM] * 2,
        out_specs=IN_VMEM,
        cost_estimate=cost(0, 1 << 20),
    )(in_vmem(mine), in_vmem(theirs))


def scalars_kernel(x, out, sem):
    copy = pltpu.make_async_copy(x, out, sem)
    copy.start()
    copy.wait()


def to_scalars(x):
    return pl.pallas_call(
        scalars_kernel,
        out_shape=SMEM(x.shape, x.dtype),
        in_specs=[IN_VMEM],
        out_specs=IN_SMEM,
        scratch_shapes=[pltpu.SemaphoreType.DMA(())],
        cost_estimate=cost(0, 1 << 20),
    )(in_vmem(x))


def tables_kernel(channels, widths, spans, bands, scale, mask):
    lag = lax.broadcasted_iota(jnp.int32, (LANES, LANES), 1) - lax.broadcasted_iota(jnp.int32, (LANES, LANES), 0)
    row = lax.broadcasted_iota(jnp.int32, (SPAN, LANES), 0)
    for n in range(widths.shape[0]):
        width = widths[n]
        cols = pl.ds(n * LANES, LANES)
        bands[:LANES, cols] = ((lag >= 0) & (lag < width)).astype(jnp.bfloat16)
        bands[LANES:, cols] = (lag + LANES < width).astype(jnp.bfloat16)
        scale[n : n + 1] = 1.0 / (jnp.sqrt(jnp.full((1, LANES), width, jnp.float32)) * (channels**0.5))
    mask[...] = (row < spans[lax.axis_index("trials")]).astype(jnp.float32)


def tables(widths, spans, channels):
    nw = widths.shape[0]
    return pl.pallas_call(
        functools.partial(tables_kernel, channels),
        out_shape=(
            VMEM((2 * LANES, nw * LANES), jnp.bfloat16),
            VMEM((nw, LANES), jnp.float32),
            VMEM((SPAN, LANES), jnp.float32),
        ),
        in_specs=[IN_SMEM] * 2,
        out_specs=(IN_VMEM,) * 3,
        cost_estimate=cost(0, 1 << 20),
    )(widths, spans)


def windows(out, raw, masks, mean, delays, row, trials, group):
    me = lax.axis_index("trials")
    for i in range(trials):
        j = i % SUBT
        acc = None
        for a, ref in enumerate(raw):
            cut = ref[j, pl.ds(delays[row, i, me ^ masks[a]], SPAN), :]
            acc = cut if acc is None else acc + cut
        less = None
        if group <= 16:
            for s in range(group):
                cut = mean[j, pl.ds(delays[row, i, s], SPAN), :]
                less = cut if less is None else less + cut
        else:
            less = lax.fori_loop(
                0, group, lambda s, v: v + mean[j, pl.ds(delays[row, i, s], SPAN), :], jnp.zeros_like(acc)
            )
        out[i] = acc - less


def near_kernel(masks, trials, group, channels, *refs):
    known = len(masks)
    raw, (near, keep, send, mean) = refs[:known], refs[known:]
    total = raw[0][0]
    for a in range(1, known):
        total = total + raw[a][0]
    mean[0] = total * (CH_SUB / channels)
    total = total * (PER_LAG / channels)
    for k in (1, 2, 4):
        total = total + shifted(total, k)
    mean[1] = total
    core = lax.axis_index("trials") & 1
    windows(keep, raw, masks, mean, near, core, trials, group)
    windows(send, raw, masks, mean, near, 1 - core, trials, group)


def near_sums(raw, masks, near, trials, group):
    one = VMEM((trials, SPAN, LANES), jnp.float32)
    return pl.pallas_call(
        functools.partial(near_kernel, masks, trials, group, CH_SUB * group),
        out_shape=(one, one, VMEM(raw[0].shape, jnp.float32)),
        in_specs=[IN_VMEM] * len(raw) + [IN_SMEM],
        out_specs=(IN_VMEM,) * 3,
        cost_estimate=cost(0, 1 << 20),
    )(*[in_vmem(r) for r in raw], in_smem(near))


def far_kernel(masks, trials, group, other, *refs):
    known = len(masks)
    raw, (mean, far_in, out, far, sem) = refs[:known], refs[known:]
    which = (lax.axis_index("trials") & 1) ^ other
    chips = out.shape[0]
    if chips == 1:
        tile = far_in[which]
        for i in range(trials):
            for s in range(group):
                far[0, i, s] = tile[i, s]
        windows(out.at[0], raw, masks, mean, far, 0, trials, group)
    else:
        copy = pltpu.make_async_copy(far_in, far, sem)
        copy.start()
        copy.wait()

        @pl.loop(0, chips)
        def _(e):
            windows(out.at[e], raw, masks, mean, far, 2 * e + which, trials, group)


def far_sums(other, raw, masks, mean, far, trials, group):
    return pl.pallas_call(
        functools.partial(far_kernel, masks, trials, group, other),
        out_shape=VMEM((far.shape[0] // 2, trials, SPAN, LANES), jnp.float32),
        in_specs=[IN_VMEM] * (len(raw) + 2),
        out_specs=IN_VMEM,
        scratch_shapes=[pltpu.SMEM(far.shape, jnp.int32), pltpu.SemaphoreType.DMA(())],
        cost_estimate=cost(0, 1 << 20),
    )(*[in_vmem(v) for v in (*raw, mean, far)])


def boxcar_kernel(a, b, bands, scale, mask, out, y, sems):
    trials = a.shape[0]
    rows = trials * SPAN
    trial = jnp.where(mask[...][None] > 0.0, a[...] + b[...], 0.0).reshape(rows, LANES)
    block = lax.broadcasted_iota(jnp.int32, trial.shape, 0) % SPAN
    before = jnp.where(block >= 1, pltpu.roll(trial, 1, 0), 0.0)
    rest = jnp.concatenate([trial, before], axis=1)
    pieces = []
    for _ in range(3):
        pieces.append(rest.astype(jnp.bfloat16))
        rest = rest - pieces[-1].astype(jnp.float32)
    sums = jnp.dot(jnp.concatenate(pieces, axis=0), bands[...], preferred_element_type=jnp.float32)
    sums = sums[:rows] + (sums[rows : 2 * rows] + sums[2 * rows :])
    copies = []
    for t in range(trials):
        for n in range(scale.shape[0]):
            y[t, :, n, :] = sums[t * SPAN : (t + 1) * SPAN, n * LANES : (n + 1) * LANES] * scale[n : n + 1]
        copies.append(pltpu.make_async_copy(y.at[t], out.at[t], sems.at[t]))
        copies[-1].start()
    for c in copies:
        c.wait()


def boxcars(a, b, bands, scale, mask):
    trials, nw = a.shape[0], scale.shape[0]
    shape = (trials, SPAN, nw, LANES)
    out = pl.pallas_call(
        boxcar_kernel,
        out_shape=jax.ShapeDtypeStruct(shape, jnp.float32),
        in_specs=[IN_VMEM] * 5,
        out_specs=pl.BlockSpec(memory_space=pl.ANY),
        scratch_shapes=[pltpu.VMEM(shape, jnp.float32), pltpu.SemaphoreType.DMA((trials,))],
        cost_estimate=cost(0, 1 << 20),
    )(*[in_vmem(v) for v in (a, b, bands, scale, mask)])
    return out.transpose(0, 2, 1, 3).reshape(trials, nw, SPAN * LANES)


def on_device(spectra, delays, spans, widths):
    group = lax.axis_size("trials")
    channels = CH_SUB * group
    trials = delays.shape[0]
    masks = (0, 2, 4, 6)
    far_bits = [b for b in (8, 16, 32, 64, 128, 256) if b < group]

    raw, rows = raw_series(spectra, delays)
    raw, theirs = lax.optimization_barrier((raw, swap(delays, 1, group)))
    raws = [raw] + [swap(raw, m, group) for m in masks[1:]]
    owned = pack_delays(rows, theirs)
    near = to_scalars(owned)
    for b in far_bits:
        owned = jnp.concatenate([owned, swap(owned, b, group)])[2 if b == far_bits[-1] else 0 :]
    boxes = tables(widths, spans, channels)

    keep, send, mean = near_sums(raws, masks, near, trials, group)
    here = keep + swap(send, 1, group)
    far = swap(far_sums(1, raws, masks, mean, owned, trials, group), 1, group)
    far = far + far_sums(0, raws, masks, mean, owned, trials, group)
    sums = jnp.concatenate([here[None], far])
    for b in reversed(far_bits):
        half = sums.shape[0] // 2
        mine, theirs = sums[:half], swap(sums[half:], b, group)
        sums = mine + theirs
    return boxcars(mine[0], theirs[0], *boxes)


def solution(mesh):
    in_specs = (P(("beams", "trials"), None), P("trials", None), P(), P())
    out_specs = P(("beams", "trials"), None, None)
    return jax.shard_map(
        on_device, mesh=mesh, in_specs=in_specs, out_specs=out_specs, check_vma=False
    )
```

```python
import functools

import jax
import jax.numpy as jnp
from jax import lax
from jax.experimental import pallas as pl
from jax.experimental.pallas import tpu as pltpu
from jax.sharding import PartitionSpec as P

CH_SUB = 128
SUBT = 2
SPAN = 8
KMAX = 8
LANES = 128
PER_LAG = CH_SUB // KMAX
VMEM = pltpu.MemorySpace.VMEM
SMEM = pltpu.MemorySpace.SMEM
IN_VMEM = pl.BlockSpec(memory_space=VMEM)
IN_SMEM = pl.BlockSpec(memory_space=SMEM)


def in_vmem(x):
    return pltpu.with_memory_space_constraint(x, VMEM)


def in_smem(x):
    return pltpu.with_memory_space_constraint(x, SMEM)


def cost(flops, read):
    return pl.CostEstimate(flops=flops, bytes_accessed=read, transcendentals=0)


def swap(x, bit, group):
    return lax.ppermute(x, "trials", [(i, i ^ bit) for i in range(group)])


def shifted(x, k):
    lane = lax.broadcasted_iota(jnp.int32, x.shape, 1)
    row = lax.broadcasted_iota(jnp.int32, x.shape, 0)
    here = pltpu.roll(x, LANES - k, 1)
    after = pltpu.roll(here, x.shape[0] - 1, 0)
    after = jnp.where(row == x.shape[0] - 1, 0.0, after)
    return jnp.where(lane < LANES - k, here, after)


def raw_kernel(chunks, x_hbm, delays_hbm, out, rows, x, delays, sems):
    blocks = x.shape[1] // LANES
    width = x.shape[1] // chunks
    copies = []
    for i in range(chunks):
        part = pl.ds(i * width, width)
        copies.append(pltpu.make_async_copy(x_hbm.at[:, part], x.at[:, part], sems.at[i]))
        copies[-1].start()
    copies.append(pltpu.make_async_copy(delays_hbm, delays, sems.at[chunks]))
    copies[-1].start()
    row = lax.broadcasted_iota(jnp.int32, (2 * KMAX, CH_SUB), 0)
    chan = lax.broadcasted_iota(jnp.int32, (2 * KMAX, CH_SUB), 1)
    select = ((row >= KMAX) | (chan // PER_LAG == KMAX - 1 - row)).astype(jnp.bfloat16)
    sub = lax.broadcasted_iota(jnp.int32, (KMAX, LANES), 0)
    lane = lax.broadcasted_iota(jnp.int32, (KMAX, LANES), 1)
    stays = lane < LANES - (KMAX - 1 - sub)
    rows[...] = jnp.zeros_like(rows)
    rolled, plain = [], []

    def finish(b0):
        first = plain[b0]
        for k in range(1, 8):
            first = jnp.where(sub == k, plain[b0 + k], first)
        out[0, b0 : b0 + 8] = first
        level = [jnp.where(stays, rolled[b], rolled[b + 1]) for b in range(b0, b0 + 8)]
        for half in (4, 2, 1):
            low = (sub & half) == 0
            level = [
                jnp.where(low, level[k] + pltpu.roll(level[k], 8 - half, 0), level[k + half] + pltpu.roll(level[k + half], half, 0))
                for k in range(half)
            ]
        out[1, b0 : b0 + 8] = level[0]

    for b0 in range(0, blocks, 8):
        if b0 * LANES % width == 0:
            copies[b0 * LANES // width].wait()
        part = x[:, b0 * LANES : (b0 + 8) * LANES]
        sums = jnp.dot(select, part, preferred_element_type=jnp.float32)
        for b in range(8):
            cut = sums[:KMAX, b * LANES : (b + 1) * LANES]
            rolled.append(pltpu.roll(cut, LANES - (KMAX - 1), 1, stride=1, stride_axis=0))
            plain.append(sums[KMAX:, b * LANES : (b + 1) * LANES])
        if b0:
            finish(b0 - 8)
    rolled.append(jnp.zeros((KMAX, LANES), jnp.float32))
    finish(blocks - 8)
    copies[chunks].wait()
    rows[: delays.shape[0], : delays.shape[1]] = delays[...]


def raw_series(spectra, delays):
    channels, samples = spectra.shape
    chunks = 2
    return pl.pallas_call(
        functools.partial(raw_kernel, chunks),
        out_shape=(VMEM((SUBT, samples // LANES, LANES), jnp.float32), VMEM((8, LANES), jnp.int32)),
        in_specs=[pl.BlockSpec(memory_space=pl.ANY)] * 2,
        out_specs=(IN_VMEM,) * 2,
        scratch_shapes=[
            pltpu.VMEM(spectra.shape, spectra.dtype),
            pltpu.VMEM(delays.shape, delays.dtype),
            pltpu.SemaphoreType.DMA((chunks + 1,)),
        ],
        cost_estimate=cost(4 * KMAX * channels * samples, 2 * channels * samples),
    )(spectra, delays)


def pass_kernel(x, out):
    out[...] = x[...]


def pass_on(x):
    return pl.pallas_call(
        pass_kernel,
        out_shape=VMEM(x.shape, x.dtype),
        in_specs=[IN_VMEM],
        out_specs=IN_VMEM,
        cost_estimate=cost(1 << 34, 1 << 24),
    )(in_vmem(x))


def tables_kernel(channels, widths, spans, bands, scale, mask):
    lag = lax.broadcasted_iota(jnp.int32, (LANES, LANES), 1) - lax.broadcasted_iota(jnp.int32, (LANES, LANES), 0)
    row = lax.broadcasted_iota(jnp.int32, (SPAN, LANES), 0)
    for n in range(widths.shape[0]):
        width = widths[n]
        cols = pl.ds(n * LANES, LANES)
        bands[:LANES, cols] = ((lag >= 0) & (lag < width)).astype(jnp.bfloat16)
        bands[LANES:, cols] = (lag + LANES < width).astype(jnp.bfloat16)
        scale[n : n + 1] = 1.0 / (jnp.sqrt(jnp.full((1, LANES), width, jnp.float32)) * (channels**0.5))
    mask[...] = (row < spans[lax.axis_index("trials")]).astype(jnp.float32)


def tables(widths, spans, channels):
    nw = widths.shape[0]
    return pl.pallas_call(
        functools.partial(tables_kernel, channels),
        out_shape=(
            VMEM((2 * LANES, nw * LANES), jnp.bfloat16),
            VMEM((nw, LANES), jnp.float32),
            VMEM((SPAN, LANES), jnp.float32),
        ),
        in_specs=[IN_SMEM] * 2,
        out_specs=(IN_VMEM,) * 3,
        cost_estimate=cost(0, 1 << 20),
    )(widths, spans)


def windows(out, raw, masks, mean, rows, delays, trials, group):
    me = lax.axis_index("trials")
    if group <= 16:
        tile = rows[...]
        for i in range(trials):
            for s in range(group):
                delays[i, s] = tile[i, s]
    else:
        pltpu.sync_copy(rows, delays)
    for i in range(trials):
        j = i % SUBT
        acc = None
        for a, ref in enumerate(raw):
            cut = ref[j, pl.ds(delays[i, me ^ masks[a]], SPAN), :]
            acc = cut if acc is None else acc + cut
        less = None
        if group <= 16:
            for s in range(group):
                cut = mean[j, pl.ds(delays[i, s], SPAN), :]
                less = cut if less is None else less + cut
        else:
            less = lax.fori_loop(
                0, group, lambda s, v: v + mean[j, pl.ds(delays[i, s], SPAN), :], jnp.zeros_like(acc)
            )
        out[i] = acc - less


def far_kernel(masks, trials, group, channels, *refs):
    known = len(masks)
    raw, (far, out, mean, delays) = refs[:known], refs[known:]
    total = raw[0][0]
    for a in range(1, known):
        total = total + raw[a][0]
    mean[0] = total * (CH_SUB / channels)
    total = total * (PER_LAG / channels)
    for k in (1, 2, 4):
        total = total + shifted(total, k)
    mean[1] = total

    def one(e):
        windows(out.at[e], raw, masks, mean, far.at[e], delays, trials, group)

    if out.shape[0] == 1:
        one(0)
    else:
        pl.loop(0, out.shape[0])(one)


def far_sums(raw, masks, far, trials, group):
    return pl.pallas_call(
        functools.partial(far_kernel, masks, trials, group, CH_SUB * group),
        out_shape=(VMEM((far.shape[0], trials, SPAN, LANES), jnp.float32), VMEM(raw[0].shape, jnp.float32)),
        in_specs=[IN_VMEM] * (len(raw) + 1),
        out_specs=(IN_VMEM,) * 2,
        scratch_shapes=[pltpu.SMEM(far.shape[1:], jnp.int32)],
        cost_estimate=cost(0, 1 << 20),
    )(*[in_vmem(v) for v in (*raw, far)])


def near_kernel(masks, trials, group, *refs):
    known = len(masks)
    raw, (mean, rows, out, delays) = refs[:known], refs[known:]
    windows(out, raw, masks, mean, rows, delays, trials, group)


def near_sums(raw, masks, mean, rows, trials, group):
    return pl.pallas_call(
        functools.partial(near_kernel, masks, trials, group),
        out_shape=VMEM((trials, SPAN, LANES), jnp.float32),
        in_specs=[IN_VMEM] * (len(raw) + 2),
        out_specs=IN_VMEM,
        scratch_shapes=[pltpu.SMEM(rows.shape, jnp.int32)],
        cost_estimate=cost(0, 1 << 20),
    )(*[in_vmem(v) for v in (*raw, mean, rows)])


def boxcar_kernel(a, b, bands, scale, mask, out, y, sems):
    trials = a.shape[0]
    rows = trials * SPAN
    trial = jnp.where(mask[...][None] > 0.0, a[...] + b[...], 0.0).reshape(rows, LANES)
    block = lax.broadcasted_iota(jnp.int32, trial.shape, 0) % SPAN
    before = jnp.where(block >= 1, pltpu.roll(trial, 1, 0), 0.0)
    rest = jnp.concatenate([trial, before], axis=1)
    pieces = []
    for _ in range(3):
        pieces.append(rest.astype(jnp.bfloat16))
        rest = rest - pieces[-1].astype(jnp.float32)
    sums = jnp.dot(jnp.concatenate(pieces, axis=0), bands[...], preferred_element_type=jnp.float32)
    sums = sums[:rows] + (sums[rows : 2 * rows] + sums[2 * rows :])
    copies = []
    for t in range(trials):
        for n in range(scale.shape[0]):
            y[t, :, n, :] = sums[t * SPAN : (t + 1) * SPAN, n * LANES : (n + 1) * LANES] * scale[n : n + 1]
        copies.append(pltpu.make_async_copy(y.at[t], out.at[t], sems.at[t]))
        copies[-1].start()
    for c in copies:
        c.wait()


def boxcars(a, b, bands, scale, mask):
    trials, nw = a.shape[0], scale.shape[0]
    shape = (trials, SPAN, nw, LANES)
    out = pl.pallas_call(
        boxcar_kernel,
        out_shape=jax.ShapeDtypeStruct(shape, jnp.float32),
        in_specs=[IN_VMEM] * 5,
        out_specs=pl.BlockSpec(memory_space=pl.ANY),
        scratch_shapes=[pltpu.VMEM(shape, jnp.float32), pltpu.SemaphoreType.DMA((trials,))],
        cost_estimate=cost(0, 1 << 20),
    )(*[in_vmem(v) for v in (a, b, bands, scale, mask)])
    return out.transpose(0, 2, 1, 3).reshape(trials, nw, SPAN * LANES)


def on_device(spectra, delays, spans, widths):
    group = lax.axis_size("trials")
    channels = CH_SUB * group
    trials = delays.shape[0]
    far_bits = [b for b in (8, 16, 32, 64, 128, 256) if b < group]

    raw, rows = raw_series(spectra, delays)
    masks = (0, 2, 4, 6)
    raws = [raw] + [swap(raw, m, group) for m in masks[1:]]
    raws = raws + [swap(r, 1, group) for r in raws]
    masks = masks + tuple(m ^ 1 for m in masks)
    owned = rows[None]
    for b in far_bits:
        owned = jnp.concatenate([owned, swap(owned, b, group)])
    boxes = tables(widths, spans, channels)

    far, mean = far_sums(raws, masks, pass_on(owned[1:]), trials, group)
    sums = jnp.concatenate([near_sums(raws, masks, mean, rows, trials, group)[None], far])
    for b in reversed(far_bits):
        half = sums.shape[0] // 2
        mine, theirs = sums[:half], swap(sums[half:], b, group)
        sums = mine + theirs
    return boxcars(mine[0], theirs[0], *boxes)


def solution(mesh):
    in_specs = (P(("beams", "trials"), None), P("trials", None), P(), P())
    out_specs = P(("beams", "trials"), None, None)
    return jax.shard_map(
        on_device, mesh=mesh, in_specs=in_specs, out_specs=out_specs, check_vma=False
    )
```

```python
import functools

import jax
import jax.numpy as jnp
from jax import lax
from jax.experimental import pallas as pl
from jax.experimental.pallas import tpu as pltpu
from jax.sharding import PartitionSpec as P

CH_SUB = 128
SUBT = 2
SPAN = 8
KMAX = 8
LANES = 128
PER_LAG = CH_SUB // KMAX
VMEM = pltpu.MemorySpace.VMEM
SMEM = pltpu.MemorySpace.SMEM
IN_VMEM = pl.BlockSpec(memory_space=VMEM)
IN_SMEM = pl.BlockSpec(memory_space=SMEM)


def in_vmem(x):
    return pltpu.with_memory_space_constraint(x, VMEM)


def in_smem(x):
    return pltpu.with_memory_space_constraint(x, SMEM)


def cost(flops, read):
    return pl.CostEstimate(flops=flops, bytes_accessed=read, transcendentals=0)


def swap(x, bit, group):
    return lax.ppermute(x, "trials", [(i, i ^ bit) for i in range(group)])


def shifted(x, k):
    lane = lax.broadcasted_iota(jnp.int32, x.shape, 1)
    row = lax.broadcasted_iota(jnp.int32, x.shape, 0)
    here = pltpu.roll(x, LANES - k, 1)
    after = pltpu.roll(here, x.shape[0] - 1, 0)
    after = jnp.where(row == x.shape[0] - 1, 0.0, after)
    return jnp.where(lane < LANES - k, here, after)


def raw_kernel(chunks, x_hbm, delays_hbm, out, rows, x, delays, sems):
    blocks = x.shape[1] // LANES
    width = x.shape[1] // chunks
    copies = []
    for i in range(chunks):
        part = pl.ds(i * width, width)
        copies.append(pltpu.make_async_copy(x_hbm.at[:, part], x.at[:, part], sems.at[i]))
        copies[-1].start()
    copies.append(pltpu.make_async_copy(delays_hbm, delays, sems.at[chunks]))
    copies[-1].start()
    row = lax.broadcasted_iota(jnp.int32, (2 * KMAX, CH_SUB), 0)
    chan = lax.broadcasted_iota(jnp.int32, (2 * KMAX, CH_SUB), 1)
    select = ((row >= KMAX) | (chan // PER_LAG == KMAX - 1 - row)).astype(jnp.bfloat16)
    sub = lax.broadcasted_iota(jnp.int32, (KMAX, LANES), 0)
    lane = lax.broadcasted_iota(jnp.int32, (KMAX, LANES), 1)
    stays = lane < LANES - (KMAX - 1 - sub)
    rows[...] = jnp.zeros_like(rows)
    rolled, plain = [], []

    def finish(b0):
        first = plain[b0]
        for k in range(1, 8):
            first = jnp.where(sub == k, plain[b0 + k], first)
        out[0, b0 : b0 + 8] = first
        level = [jnp.where(stays, rolled[b], rolled[b + 1]) for b in range(b0, b0 + 8)]
        for half in (4, 2, 1):
            low = (sub & half) == 0
            level = [
                jnp.where(low, level[k] + pltpu.roll(level[k], 8 - half, 0), level[k + half] + pltpu.roll(level[k + half], half, 0))
                for k in range(half)
            ]
        out[1, b0 : b0 + 8] = level[0]

    for b0 in range(0, blocks, 8):
        if b0 * LANES % width == 0:
            copies[b0 * LANES // width].wait()
        part = x[:, b0 * LANES : (b0 + 8) * LANES]
        sums = jnp.dot(select, part, preferred_element_type=jnp.float32)
        for b in range(8):
            cut = sums[:KMAX, b * LANES : (b + 1) * LANES]
            rolled.append(pltpu.roll(cut, LANES - (KMAX - 1), 1, stride=1, stride_axis=0))
            plain.append(sums[KMAX:, b * LANES : (b + 1) * LANES])
        if b0:
            finish(b0 - 8)
    rolled.append(jnp.zeros((KMAX, LANES), jnp.float32))
    finish(blocks - 8)
    copies[chunks].wait()
    rows[: delays.shape[0], : delays.shape[1]] = delays[...]


def raw_series(spectra, delays):
    channels, samples = spectra.shape
    chunks = 2
    return pl.pallas_call(
        functools.partial(raw_kernel, chunks),
        out_shape=(VMEM((SUBT, samples // LANES, LANES), jnp.float32), VMEM((8, LANES), jnp.int32)),
        in_specs=[pl.BlockSpec(memory_space=pl.ANY)] * 2,
        out_specs=(IN_VMEM,) * 2,
        scratch_shapes=[
            pltpu.VMEM(spectra.shape, spectra.dtype),
            pltpu.VMEM(delays.shape, delays.dtype),
            pltpu.SemaphoreType.DMA((chunks + 1,)),
        ],
        cost_estimate=cost(4 * KMAX * channels * samples, 2 * channels * samples),
    )(spectra, delays)


def scalars_kernel(trials, group, x, out):
    if x.shape[0] * group <= 16:
        for e in range(x.shape[0]):
            tile = x[e]
            for i in range(trials):
                for s in range(group):
                    out[e, i, s] = tile[i, s]
    else:
        pltpu.sync_copy(x, out)


def to_scalars(x, trials, group, estimate):
    return pl.pallas_call(
        functools.partial(scalars_kernel, trials, group),
        out_shape=SMEM(x.shape, x.dtype),
        in_specs=[IN_VMEM],
        out_specs=IN_SMEM,
        cost_estimate=estimate,
    )(in_vmem(x))


def tables_kernel(channels, widths, spans, bands, scale, mask):
    lag = lax.broadcasted_iota(jnp.int32, (LANES, LANES), 1) - lax.broadcasted_iota(jnp.int32, (LANES, LANES), 0)
    row = lax.broadcasted_iota(jnp.int32, (SPAN, LANES), 0)
    for n in range(widths.shape[0]):
        width = widths[n]
        cols = pl.ds(n * LANES, LANES)
        bands[:LANES, cols] = ((lag >= 0) & (lag < width)).astype(jnp.bfloat16)
        bands[LANES:, cols] = (lag + LANES < width).astype(jnp.bfloat16)
        scale[n : n + 1] = 1.0 / (jnp.sqrt(jnp.full((1, LANES), width, jnp.float32)) * (channels**0.5))
    mask[...] = (row < spans[lax.axis_index("trials")]).astype(jnp.float32)


def tables(widths, spans, channels):
    nw = widths.shape[0]
    return pl.pallas_call(
        functools.partial(tables_kernel, channels),
        out_shape=(
            VMEM((2 * LANES, nw * LANES), jnp.bfloat16),
            VMEM((nw, LANES), jnp.float32),
            VMEM((SPAN, LANES), jnp.float32),
        ),
        in_specs=[IN_SMEM] * 2,
        out_specs=(IN_VMEM,) * 3,
        cost_estimate=cost(0, 1 << 20),
    )(widths, spans)


def windows(out, raw, masks, mean, delays, e, trials, group):
    me = lax.axis_index("trials")
    for i in range(trials):
        j = i % SUBT
        acc = None
        for a, ref in enumerate(raw):
            cut = ref[j, pl.ds(delays[e, i, me ^ masks[a]], SPAN), :]
            acc = cut if acc is None else acc + cut
        less = None
        if group <= 16:
            for s in range(group):
                cut = mean[j, pl.ds(delays[e, i, s], SPAN), :]
                less = cut if less is None else less + cut
        else:
            less = lax.fori_loop(
                0, group, lambda s, v: v + mean[j, pl.ds(delays[e, i, s], SPAN), :], jnp.zeros_like(acc)
            )
        out[i] = acc - less


def far_kernel(masks, trials, group, channels, *refs):
    known = len(masks)
    raw, (far, out, mean) = refs[:known], refs[known:]
    total = raw[0][0]
    for a in range(1, known):
        total = total + raw[a][0]
    mean[0] = total * (CH_SUB / channels)
    total = total * (PER_LAG / channels)
    for k in (1, 2, 4):
        total = total + shifted(total, k)
    mean[1] = total

    def one(e):
        windows(out.at[e], raw, masks, mean, far, e, trials, group)

    if out.shape[0] == 1:
        one(0)
    else:
        pl.loop(0, out.shape[0])(one)


def far_sums(raw, masks, far, trials, group):
    return pl.pallas_call(
        functools.partial(far_kernel, masks, trials, group, CH_SUB * group),
        out_shape=(VMEM((far.shape[0], trials, SPAN, LANES), jnp.float32), VMEM(raw[0].shape, jnp.float32)),
        in_specs=[IN_VMEM] * len(raw) + [IN_SMEM],
        out_specs=(IN_VMEM,) * 2,
        cost_estimate=cost(0, 1 << 20),
    )(*[in_vmem(v) for v in raw], in_smem(far))


def near_kernel(masks, trials, group, *refs):
    known = len(masks)
    raw, (mean, near, out) = refs[:known], refs[known:]
    windows(out, raw, masks, mean, near, 0, trials, group)


def near_sums(raw, masks, mean, near, trials, group):
    return pl.pallas_call(
        functools.partial(near_kernel, masks, trials, group),
        out_shape=VMEM((trials, SPAN, LANES), jnp.float32),
        in_specs=[IN_VMEM] * (len(raw) + 1) + [IN_SMEM],
        out_specs=IN_VMEM,
        cost_estimate=cost(0, 1 << 20),
    )(*[in_vmem(v) for v in (*raw, mean)], in_smem(near))


def boxcar_kernel(a, b, bands, scale, mask, out, y, sems):
    trials = a.shape[0]
    rows = trials * SPAN
    trial = jnp.where(mask[...][None] > 0.0, a[...] + b[...], 0.0).reshape(rows, LANES)
    block = lax.broadcasted_iota(jnp.int32, trial.shape, 0) % SPAN
    before = jnp.where(block >= 1, pltpu.roll(trial, 1, 0), 0.0)
    rest = jnp.concatenate([trial, before], axis=1)
    pieces = []
    for _ in range(3):
        pieces.append(rest.astype(jnp.bfloat16))
        rest = rest - pieces[-1].astype(jnp.float32)
    sums = jnp.dot(jnp.concatenate(pieces, axis=0), bands[...], preferred_element_type=jnp.float32)
    sums = sums[:rows] + (sums[rows : 2 * rows] + sums[2 * rows :])
    copies = []
    for t in range(trials):
        for n in range(scale.shape[0]):
            y[t, :, n, :] = sums[t * SPAN : (t + 1) * SPAN, n * LANES : (n + 1) * LANES] * scale[n : n + 1]
        copies.append(pltpu.make_async_copy(y.at[t], out.at[t], sems.at[t]))
        copies[-1].start()
    for c in copies:
        c.wait()


def boxcars(a, b, bands, scale, mask):
    trials, nw = a.shape[0], scale.shape[0]
    shape = (trials, SPAN, nw, LANES)
    out = pl.pallas_call(
        boxcar_kernel,
        out_shape=jax.ShapeDtypeStruct(shape, jnp.float32),
        in_specs=[IN_VMEM] * 5,
        out_specs=pl.BlockSpec(memory_space=pl.ANY),
        scratch_shapes=[pltpu.VMEM(shape, jnp.float32), pltpu.SemaphoreType.DMA((trials,))],
        cost_estimate=cost(0, 1 << 20),
    )(*[in_vmem(v) for v in (a, b, bands, scale, mask)])
    return out.transpose(0, 2, 1, 3).reshape(trials, nw, SPAN * LANES)


def on_device(spectra, delays, spans, widths):
    group = lax.axis_size("trials")
    channels = CH_SUB * group
    trials = delays.shape[0]
    far_bits = [b for b in (8, 16, 32, 64, 128, 256) if b < group]

    raw, rows = raw_series(spectra, delays)
    masks = (0, 2, 4, 6)
    raws = [raw] + [swap(raw, m, group) for m in masks[1:]]
    raws = raws + [swap(r, 1, group) for r in raws]
    masks = masks + tuple(m ^ 1 for m in masks)
    owned = rows[None]
    for b in far_bits:
        owned = jnp.concatenate([owned, swap(owned, b, group)])
    boxes = tables(widths, spans, channels)

    near = to_scalars(rows[None], trials, group, cost(0, 1 << 20))
    away = to_scalars(owned[1:], trials, group, cost(1 << 34, 1 << 24))
    far, mean = far_sums(raws, masks, away, trials, group)
    sums = jnp.concatenate([near_sums(raws, masks, mean, near, trials, group)[None], far])
    for b in reversed(far_bits):
        half = sums.shape[0] // 2
        mine, theirs = sums[:half], swap(sums[half:], b, group)
        sums = mine + theirs
    return boxcars(mine[0], theirs[0], *boxes)


def solution(mesh):
    in_specs = (P(("beams", "trials"), None), P("trials", None), P(), P())
    out_specs = P(("beams", "trials"), None, None)
    return jax.shard_map(
        on_device, mesh=mesh, in_specs=in_specs, out_specs=out_specs, check_vma=False
    )
```

```python
import functools

import jax
import jax.numpy as jnp
from jax import lax
from jax.experimental import pallas as pl
from jax.experimental.pallas import tpu as pltpu
from jax.sharding import PartitionSpec as P

CH_SUB = 128
SUBT = 2
SPAN = 8
KMAX = 8
LANES = 128
PER_LAG = CH_SUB // KMAX
VMEM = pltpu.MemorySpace.VMEM
SMEM = pltpu.MemorySpace.SMEM
IN_VMEM = pl.BlockSpec(memory_space=VMEM)
IN_SMEM = pl.BlockSpec(memory_space=SMEM)


def in_vmem(x):
    return pltpu.with_memory_space_constraint(x, VMEM)


def in_smem(x):
    return pltpu.with_memory_space_constraint(x, SMEM)


def cost(flops, read):
    return pl.CostEstimate(flops=flops, bytes_accessed=read, transcendentals=0)


def swap(x, bit, group):
    return lax.ppermute(x, "trials", [(i, i ^ bit) for i in range(group)])


def sum_ahead(x):
    lane = lax.broadcasted_iota(jnp.int32, x.shape, 1)
    row = lax.broadcasted_iota(jnp.int32, x.shape, 0)
    after = jnp.where(row == x.shape[0] - 1, 0.0, pltpu.roll(x, x.shape[0] - 1, 0))
    for k in (1, 2, 4):
        ahead = pltpu.roll(after, LANES - k, 1)
        x = x + jnp.where(lane < LANES - k, pltpu.roll(x, LANES - k, 1), ahead)
        after = after + ahead
    return x


def raw_kernel(chunks, x_hbm, delays_hbm, out, rows, x, delays, sems):
    blocks = x.shape[1] // LANES
    width = x.shape[1] // chunks
    copies = []
    for i in range(chunks):
        part = pl.ds(i * width, width)
        copies.append(pltpu.make_async_copy(x_hbm.at[:, part], x.at[:, part], sems.at[i]))
        copies[-1].start()
    copies.append(pltpu.make_async_copy(delays_hbm, delays, sems.at[chunks]))
    copies[-1].start()
    row = lax.broadcasted_iota(jnp.int32, (2 * KMAX, CH_SUB), 0)
    chan = lax.broadcasted_iota(jnp.int32, (2 * KMAX, CH_SUB), 1)
    select = ((row >= KMAX) | (chan // PER_LAG == KMAX - 1 - row)).astype(jnp.bfloat16)
    sub = lax.broadcasted_iota(jnp.int32, (KMAX, LANES), 0)
    lane = lax.broadcasted_iota(jnp.int32, (KMAX, LANES), 1)
    stays = lane < LANES - (KMAX - 1 - sub)
    rows[...] = jnp.zeros_like(rows)
    rolled, plain = [], []

    def finish(b0):
        first = plain[b0]
        for k in range(1, 8):
            first = jnp.where(sub == k, plain[b0 + k], first)
        out[0, b0 : b0 + 8] = first
        level = [jnp.where(stays, rolled[b], rolled[b + 1]) for b in range(b0, b0 + 8)]
        for half in (4, 2, 1):
            low = (sub & half) == 0
            level = [
                jnp.where(low, level[k] + pltpu.roll(level[k], 8 - half, 0), level[k + half] + pltpu.roll(level[k + half], half, 0))
                for k in range(half)
            ]
        out[1, b0 : b0 + 8] = level[0]

    for b0 in range(0, blocks, 8):
        if b0 * LANES % width == 0:
            copies[b0 * LANES // width].wait()
        part = x[:, b0 * LANES : (b0 + 8) * LANES]
        sums = jnp.dot(select, part, preferred_element_type=jnp.float32)
        for b in range(8):
            cut = sums[:KMAX, b * LANES : (b + 1) * LANES]
            rolled.append(pltpu.roll(cut, LANES - (KMAX - 1), 1, stride=1, stride_axis=0))
            plain.append(sums[KMAX:, b * LANES : (b + 1) * LANES])
        if b0:
            finish(b0 - 8)
    rolled.append(jnp.zeros((KMAX, LANES), jnp.float32))
    finish(blocks - 8)
    copies[chunks].wait()
    rows[: delays.shape[0], : delays.shape[1]] = delays[...]


def raw_series(spectra, delays):
    channels, samples = spectra.shape
    chunks = 2
    return pl.pallas_call(
        functools.partial(raw_kernel, chunks),
        out_shape=(VMEM((SUBT, samples // LANES, LANES), jnp.float32), VMEM((8, LANES), jnp.int32)),
        in_specs=[pl.BlockSpec(memory_space=pl.ANY)] * 2,
        out_specs=(IN_VMEM,) * 2,
        scratch_shapes=[
            pltpu.VMEM(spectra.shape, spectra.dtype),
            pltpu.VMEM(delays.shape, delays.dtype),
            pltpu.SemaphoreType.DMA((chunks + 1,)),
        ],
        cost_estimate=cost(4 * KMAX * channels * samples, 2 * channels * samples),
    )(spectra, delays)


def scalars_kernel(trials, group, x, out):
    if x.shape[0] * group <= 16:
        for e in range(x.shape[0]):
            tile = x[e]
            for i in range(trials):
                for s in range(group):
                    out[e, i, s] = tile[i, s]
    else:
        pltpu.sync_copy(x, out)


def to_scalars(x, trials, group, estimate):
    return pl.pallas_call(
        functools.partial(scalars_kernel, trials, group),
        out_shape=SMEM(x.shape, x.dtype),
        in_specs=[IN_VMEM],
        out_specs=IN_SMEM,
        cost_estimate=estimate,
    )(in_vmem(x))


def tables_kernel(channels, widths, spans, bands, scale, mask):
    lag = lax.broadcasted_iota(jnp.int32, (LANES, LANES), 1) - lax.broadcasted_iota(jnp.int32, (LANES, LANES), 0)
    row = lax.broadcasted_iota(jnp.int32, (SPAN, LANES), 0)
    for n in range(widths.shape[0]):
        width = widths[n]
        cols = pl.ds(n * LANES, LANES)
        bands[:LANES, cols] = ((lag >= 0) & (lag < width)).astype(jnp.bfloat16)
        bands[LANES:, cols] = (lag + LANES < width).astype(jnp.bfloat16)
        scale[n : n + 1] = 1.0 / (jnp.sqrt(jnp.full((1, LANES), width, jnp.float32)) * (channels**0.5))
    mask[...] = (row < spans[lax.axis_index("trials")]).astype(jnp.float32)


def tables(widths, spans, channels):
    nw = widths.shape[0]
    return pl.pallas_call(
        functools.partial(tables_kernel, channels),
        out_shape=(
            VMEM((2 * LANES, nw * LANES), jnp.bfloat16),
            VMEM((nw, LANES), jnp.float32),
            VMEM((SPAN, LANES), jnp.float32),
        ),
        in_specs=[IN_SMEM] * 2,
        out_specs=(IN_VMEM,) * 3,
        cost_estimate=cost(0, 1 << 20),
    )(widths, spans)


def tree_sum(terms):
    while len(terms) > 1:
        terms = [terms[k] + terms[k + 1] for k in range(0, len(terms) - 1, 2)] + terms[len(terms) & ~1 :]
    return terms[0]


def windows(out, raw, masks, mean, delays, e, trials, group):
    me = lax.axis_index("trials")
    for i in range(trials):
        j = i % SUBT
        acc = tree_sum(
            [ref[j, pl.ds(delays[e, i, me ^ masks[a]], SPAN), :] for a, ref in enumerate(raw)]
        )
        if group <= 16:
            less = tree_sum([mean[j, pl.ds(delays[e, i, s], SPAN), :] for s in range(group)])
        else:
            less = lax.fori_loop(
                0, group, lambda s, v: v + mean[j, pl.ds(delays[e, i, s], SPAN), :], jnp.zeros_like(acc)
            )
        out[i] = acc - less


def means(total, channels):
    return total * (CH_SUB / channels), sum_ahead(total * (PER_LAG / channels))


def early_kernel(channels, *refs):
    raw, out = refs[:-1], refs[-1]
    total = raw[0][0]
    for r in raw[1:]:
        total = total + r[0]
    out[0], out[1] = means(total, channels)


def early_mean(raw, group):
    return pl.pallas_call(
        functools.partial(early_kernel, CH_SUB * group),
        out_shape=VMEM(raw[0].shape, jnp.float32),
        in_specs=[IN_VMEM] * len(raw),
        out_specs=IN_VMEM,
        cost_estimate=cost(0, 1 << 20),
    )(*[in_vmem(v) for v in raw])


def far_kernel(masks, trials, group, channels, last, *refs):
    known = len(masks)
    raw, (early, far, out, mean) = refs[:known], refs[known:]
    plain, ahead = means(raw[last][0], channels)
    mean[0] = early[0] + plain
    mean[1] = early[1] + ahead

    def one(e):
        windows(out.at[e], raw, masks, mean, far, e, trials, group)

    if out.shape[0] == 1:
        one(0)
    else:
        pl.loop(0, out.shape[0])(one)


def far_sums(raw, masks, early, last, far, trials, group):
    return pl.pallas_call(
        functools.partial(far_kernel, masks, trials, group, CH_SUB * group, last),
        out_shape=(VMEM((far.shape[0], trials, SPAN, LANES), jnp.float32), VMEM(raw[0].shape, jnp.float32)),
        in_specs=[IN_VMEM] * (len(raw) + 1) + [IN_SMEM],
        out_specs=(IN_VMEM,) * 2,
        cost_estimate=cost(0, 1 << 20),
    )(*[in_vmem(v) for v in (*raw, early)], in_smem(far))


def near_kernel(masks, trials, group, *refs):
    known = len(masks)
    raw, (mean, near, out) = refs[:known], refs[known:]
    windows(out, raw, masks, mean, near, 0, trials, group)


def near_sums(raw, masks, mean, near, trials, group):
    return pl.pallas_call(
        functools.partial(near_kernel, masks, trials, group),
        out_shape=VMEM((trials, SPAN, LANES), jnp.float32),
        in_specs=[IN_VMEM] * (len(raw) + 1) + [IN_SMEM],
        out_specs=IN_VMEM,
        cost_estimate=cost(0, 1 << 20),
    )(*[in_vmem(v) for v in (*raw, mean)], in_smem(near))


def boxcar_kernel(a, b, bands, scale, mask, out, y, sems):
    trials = a.shape[0]
    rows = trials * SPAN
    trial = jnp.where(mask[...][None] > 0.0, a[...] + b[...], 0.0).reshape(rows, LANES)
    block = lax.broadcasted_iota(jnp.int32, trial.shape, 0) % SPAN
    before = jnp.where(block >= 1, pltpu.roll(trial, 1, 0), 0.0)
    rest = jnp.concatenate([trial, before], axis=1)
    pieces = []
    for _ in range(3):
        pieces.append(rest.astype(jnp.bfloat16))
        rest = rest - pieces[-1].astype(jnp.float32)
    sums = jnp.dot(jnp.concatenate(pieces, axis=0), bands[...], preferred_element_type=jnp.float32)
    sums = sums[:rows] + (sums[rows : 2 * rows] + sums[2 * rows :])
    copies = []
    for t in range(trials):
        for n in range(scale.shape[0]):
            y[t, :, n, :] = sums[t * SPAN : (t + 1) * SPAN, n * LANES : (n + 1) * LANES] * scale[n : n + 1]
        copies.append(pltpu.make_async_copy(y.at[t], out.at[t], sems.at[t]))
        copies[-1].start()
    for c in copies:
        c.wait()


def boxcars(a, b, bands, scale, mask):
    trials, nw = a.shape[0], scale.shape[0]
    shape = (trials, SPAN, nw, LANES)
    out = pl.pallas_call(
        boxcar_kernel,
        out_shape=jax.ShapeDtypeStruct(shape, jnp.float32),
        in_specs=[IN_VMEM] * 5,
        out_specs=pl.BlockSpec(memory_space=pl.ANY),
        scratch_shapes=[pltpu.VMEM(shape, jnp.float32), pltpu.SemaphoreType.DMA((trials,))],
        cost_estimate=cost(0, 1 << 20),
    )(*[in_vmem(v) for v in (a, b, bands, scale, mask)])
    return out.transpose(0, 2, 1, 3).reshape(trials, nw, SPAN * LANES)


def on_device(spectra, delays, spans, widths):
    group = lax.axis_size("trials")
    channels = CH_SUB * group
    trials = delays.shape[0]
    far_bits = [b for b in (8, 16, 32, 64, 128, 256) if b < group]

    raw, rows = raw_series(spectra, delays)
    masks = (0, 2, 4, 6)
    raws = [raw] + [swap(raw, m, group) for m in masks[1:]]
    raws = raws + [swap(r, 1, group) for r in raws]
    masks = masks + tuple(m ^ 1 for m in masks)
    owned = rows[None]
    for b in far_bits:
        owned = jnp.concatenate([owned, swap(owned, b, group)])
    boxes = tables(widths, spans, channels)

    near = to_scalars(rows[None], trials, group, cost(0, 1 << 20))
    away = to_scalars(owned[1:], trials, group, cost(1 << 34, 1 << 24))
    last = masks.index(3)
    early = early_mean(raws[:last] + raws[last + 1 :], group)
    far, mean = far_sums(raws, masks, early, last, away, trials, group)
    sums = jnp.concatenate([near_sums(raws, masks, mean, near, trials, group)[None], far])
    for b in reversed(far_bits):
        half = sums.shape[0] // 2
        mine, theirs = sums[:half], swap(sums[half:], b, group)
        sums = mine + theirs
    return boxcars(mine[0], theirs[0], *boxes)


def solution(mesh):
    in_specs = (P(("beams", "trials"), None), P("trials", None), P(), P())
    out_specs = P(("beams", "trials"), None, None)
    return jax.shard_map(
        on_device, mesh=mesh, in_specs=in_specs, out_specs=out_specs, check_vma=False
    )
```

```python
import functools

import jax
import jax.numpy as jnp
from jax import lax
from jax.experimental import pallas as pl
from jax.experimental.pallas import tpu as pltpu
from jax.sharding import PartitionSpec as P

CH_SUB = 128
SUBT = 2
SPAN = 8
KMAX = 8
LANES = 128
PER_LAG = CH_SUB // KMAX
VMEM = pltpu.MemorySpace.VMEM
SMEM = pltpu.MemorySpace.SMEM
IN_VMEM = pl.BlockSpec(memory_space=VMEM)
IN_SMEM = pl.BlockSpec(memory_space=SMEM)


def in_vmem(x):
    return pltpu.with_memory_space_constraint(x, VMEM)


def in_smem(x):
    return pltpu.with_memory_space_constraint(x, SMEM)


def cost(flops, read):
    return pl.CostEstimate(flops=flops, bytes_accessed=read, transcendentals=0)


def swap(x, bit, group):
    return lax.ppermute(x, "trials", [(i, i ^ bit) for i in range(group)])


def shifted(x, k):
    lane = lax.broadcasted_iota(jnp.int32, x.shape, 1)
    row = lax.broadcasted_iota(jnp.int32, x.shape, 0)
    here = pltpu.roll(x, LANES - k, 1)
    after = pltpu.roll(here, x.shape[0] - 1, 0)
    after = jnp.where(row == x.shape[0] - 1, 0.0, after)
    return jnp.where(lane < LANES - k, here, after)


def raw_kernel(chunks, x_hbm, delays_hbm, out, rows, x, delays, sems):
    blocks = x.shape[1] // LANES
    width = x.shape[1] // chunks
    copies = []
    for i in range(chunks):
        part = pl.ds(i * width, width)
        copies.append(pltpu.make_async_copy(x_hbm.at[:, part], x.at[:, part], sems.at[i]))
        copies[-1].start()
    copies.append(pltpu.make_async_copy(delays_hbm, delays, sems.at[chunks]))
    copies[-1].start()
    row = lax.broadcasted_iota(jnp.int32, (2 * KMAX, CH_SUB), 0)
    chan = lax.broadcasted_iota(jnp.int32, (2 * KMAX, CH_SUB), 1)
    select = ((row >= KMAX) | (chan // PER_LAG == KMAX - 1 - row)).astype(jnp.bfloat16)
    sub = lax.broadcasted_iota(jnp.int32, (KMAX, LANES), 0)
    lane = lax.broadcasted_iota(jnp.int32, (KMAX, LANES), 1)
    stays = lane < LANES - (KMAX - 1 - sub)
    rows[...] = jnp.zeros_like(rows)
    rolled, plain = [], []

    def finish(b0):
        first = plain[b0]
        for k in range(1, 8):
            first = jnp.where(sub == k, plain[b0 + k], first)
        out[0, b0 : b0 + 8] = first
        level = [jnp.where(stays, rolled[b], rolled[b + 1]) for b in range(b0, b0 + 8)]
        for half in (4, 2, 1):
            low = (sub & half) == 0
            level = [
                jnp.where(low, level[k] + pltpu.roll(level[k], 8 - half, 0), level[k + half] + pltpu.roll(level[k + half], half, 0))
                for k in range(half)
            ]
        out[1, b0 : b0 + 8] = level[0]

    for b0 in range(0, blocks, 8):
        if b0 * LANES % width == 0:
            copies[b0 * LANES // width].wait()
        part = x[:, b0 * LANES : (b0 + 8) * LANES]
        sums = jnp.dot(select, part, preferred_element_type=jnp.float32)
        for b in range(8):
            cut = sums[:KMAX, b * LANES : (b + 1) * LANES]
            rolled.append(pltpu.roll(cut, LANES - (KMAX - 1), 1, stride=1, stride_axis=0))
            plain.append(sums[KMAX:, b * LANES : (b + 1) * LANES])
        if b0:
            finish(b0 - 8)
    rolled.append(jnp.zeros((KMAX, LANES), jnp.float32))
    finish(blocks - 8)
    copies[chunks].wait()
    rows[: delays.shape[0], : delays.shape[1]] = delays[...]


def raw_series(spectra, delays):
    channels, samples = spectra.shape
    chunks = 2
    return pl.pallas_call(
        functools.partial(raw_kernel, chunks),
        out_shape=(VMEM((SUBT, samples // LANES, LANES), jnp.float32), VMEM((8, LANES), jnp.int32)),
        in_specs=[pl.BlockSpec(memory_space=pl.ANY)] * 2,
        out_specs=(IN_VMEM,) * 2,
        scratch_shapes=[
            pltpu.VMEM(spectra.shape, spectra.dtype),
            pltpu.VMEM(delays.shape, delays.dtype),
            pltpu.SemaphoreType.DMA((chunks + 1,)),
        ],
        cost_estimate=cost(4 * KMAX * channels * samples, 2 * channels * samples),
    )(spectra, delays)


def scalars_kernel(trials, group, x, out):
    if x.shape[0] * group <= 16:
        for e in range(x.shape[0]):
            tile = x[e]
            for i in range(trials):
                for s in range(group):
                    out[e, i, s] = tile[i, s]
    else:
        pltpu.sync_copy(x, out)


def to_scalars(x, trials, group, estimate):
    return pl.pallas_call(
        functools.partial(scalars_kernel, trials, group),
        out_shape=SMEM(x.shape, x.dtype),
        in_specs=[IN_VMEM],
        out_specs=IN_SMEM,
        cost_estimate=estimate,
    )(in_vmem(x))


def tables_kernel(channels, widths, spans, bands, scale, mask):
    lag = lax.broadcasted_iota(jnp.int32, (LANES, LANES), 1) - lax.broadcasted_iota(jnp.int32, (LANES, LANES), 0)
    row = lax.broadcasted_iota(jnp.int32, (SPAN, LANES), 0)
    for n in range(widths.shape[0]):
        width = widths[n]
        cols = pl.ds(n * LANES, LANES)
        bands[:LANES, cols] = ((lag >= 0) & (lag < width)).astype(jnp.bfloat16)
        bands[LANES:, cols] = (lag + LANES < width).astype(jnp.bfloat16)
        scale[n : n + 1] = 1.0 / (jnp.sqrt(jnp.full((1, LANES), width, jnp.float32)) * (channels**0.5))
    mask[...] = (row < spans[lax.axis_index("trials")]).astype(jnp.float32)


def tables(widths, spans, channels):
    nw = widths.shape[0]
    return pl.pallas_call(
        functools.partial(tables_kernel, channels),
        out_shape=(
            VMEM((2 * LANES, nw * LANES), jnp.bfloat16),
            VMEM((nw, LANES), jnp.float32),
            VMEM((SPAN, LANES), jnp.float32),
        ),
        in_specs=[IN_SMEM] * 2,
        out_specs=(IN_VMEM,) * 3,
        cost_estimate=cost(0, 1 << 20),
    )(widths, spans)


def windows(out, raw, masks, mean, delays, e, trials, group):
    me = lax.axis_index("trials")
    for i in range(trials):
        j = i % SUBT
        acc = None
        for a, ref in enumerate(raw):
            cut = ref[j, pl.ds(delays[e, i, me ^ masks[a]], SPAN), :]
            acc = cut if acc is None else acc + cut
        less = None
        if group <= 16:
            for s in range(group):
                cut = mean[j, pl.ds(delays[e, i, s], SPAN), :]
                less = cut if less is None else less + cut
        else:
            less = lax.fori_loop(
                0, group, lambda s, v: v + mean[j, pl.ds(delays[e, i, s], SPAN), :], jnp.zeros_like(acc)
            )
        out[i] = acc - less


def far_kernel(masks, trials, group, channels, *refs):
    known = len(masks)
    raw, (far, out, mean) = refs[:known], refs[known:]
    total = raw[0][0]
    for a in range(1, known):
        total = total + raw[a][0]
    mean[0] = total * (CH_SUB / channels)
    total = total * (PER_LAG / channels)
    for k in (1, 2, 4):
        total = total + shifted(total, k)
    mean[1] = total

    def one(e):
        windows(out.at[e], raw, masks, mean, far, e, trials, group)

    if out.shape[0] == 1:
        one(0)
    else:
        pl.loop(0, out.shape[0])(one)


def far_sums(raw, masks, far, trials, group):
    return pl.pallas_call(
        functools.partial(far_kernel, masks, trials, group, CH_SUB * group),
        out_shape=(VMEM((far.shape[0], trials, SPAN, LANES), jnp.float32), VMEM(raw[0].shape, jnp.float32)),
        in_specs=[IN_VMEM] * len(raw) + [IN_SMEM],
        out_specs=(IN_VMEM,) * 2,
        cost_estimate=cost(0, 1 << 20),
    )(*[in_vmem(v) for v in raw], in_smem(far))


def near_kernel(masks, trials, group, *refs):
    known = len(masks)
    raw, (mean, near, out) = refs[:known], refs[known:]
    windows(out, raw, masks, mean, near, 0, trials, group)


def near_sums(raw, masks, mean, near, trials, group):
    return pl.pallas_call(
        functools.partial(near_kernel, masks, trials, group),
        out_shape=VMEM((trials, SPAN, LANES), jnp.float32),
        in_specs=[IN_VMEM] * (len(raw) + 1) + [IN_SMEM],
        out_specs=IN_VMEM,
        cost_estimate=cost(0, 1 << 20),
    )(*[in_vmem(v) for v in (*raw, mean)], in_smem(near))


def boxcar_kernel(a, b, bands, scale, mask, out, y, sems):
    trials = a.shape[0]
    rows = trials * SPAN
    trial = jnp.where(mask[...][None] > 0.0, a[...] + b[...], 0.0).reshape(rows, LANES)
    block = lax.broadcasted_iota(jnp.int32, trial.shape, 0) % SPAN
    before = jnp.where(block >= 1, pltpu.roll(trial, 1, 0), 0.0)
    rest = jnp.concatenate([trial, before], axis=1)
    pieces = []
    for _ in range(3):
        pieces.append(rest.astype(jnp.bfloat16))
        rest = rest - pieces[-1].astype(jnp.float32)
    sums = jnp.dot(jnp.concatenate(pieces, axis=0), bands[...], preferred_element_type=jnp.float32)
    sums = sums[:rows] + (sums[rows : 2 * rows] + sums[2 * rows :])
    copies = []
    for t in range(trials):
        for n in range(scale.shape[0]):
            y[t, :, n, :] = sums[t * SPAN : (t + 1) * SPAN, n * LANES : (n + 1) * LANES] * scale[n : n + 1]
        copies.append(pltpu.make_async_copy(y.at[t], out.at[t], sems.at[t]))
        copies[-1].start()
    for c in copies:
        c.wait()


def boxcars(a, b, bands, scale, mask):
    trials, nw = a.shape[0], scale.shape[0]
    shape = (trials, SPAN, nw, LANES)
    out = pl.pallas_call(
        boxcar_kernel,
        out_shape=jax.ShapeDtypeStruct(shape, jnp.float32),
        in_specs=[IN_VMEM] * 5,
        out_specs=pl.BlockSpec(memory_space=pl.ANY),
        scratch_shapes=[pltpu.VMEM(shape, jnp.float32), pltpu.SemaphoreType.DMA((trials,))],
        cost_estimate=cost(0, 1 << 20),
    )(*[in_vmem(v) for v in (a, b, bands, scale, mask)])
    return out.transpose(0, 2, 1, 3).reshape(trials, nw, SPAN * LANES)


def on_device(spectra, delays, spans, widths):
    group = lax.axis_size("trials")
    channels = CH_SUB * group
    trials = delays.shape[0]
    far_bits = [b for b in (8, 16, 32, 64, 128, 256) if b < group]

    raw, rows = raw_series(spectra, delays)
    masks = (0, 2, 4, 7)
    raws = [raw] + [swap(raw, m, group) for m in masks[1:]]
    raws = raws + [swap(r, 1, group) for r in raws]
    masks = masks + tuple(m ^ 1 for m in masks)
    owned = rows[None]
    for b in far_bits:
        owned = jnp.concatenate([owned, swap(owned, b, group)])
    boxes = tables(widths, spans, channels)

    near = to_scalars(rows[None], trials, group, cost(0, 1 << 20))
    away = to_scalars(owned[1:], trials, group, cost(1 << 34, 1 << 24))
    far, mean = far_sums(raws, masks, away, trials, group)
    sums = jnp.concatenate([near_sums(raws, masks, mean, near, trials, group)[None], far])
    for b in reversed(far_bits):
        half = sums.shape[0] // 2
        mine, theirs = sums[:half], swap(sums[half:], b, group)
        sums = mine + theirs
    return boxcars(mine[0], theirs[0], *boxes)


def solution(mesh):
    in_specs = (P(("beams", "trials"), None), P("trials", None), P(), P())
    out_specs = P(("beams", "trials"), None, None)
    return jax.shard_map(
        on_device, mesh=mesh, in_specs=in_specs, out_specs=out_specs, check_vma=False
    )
```

```python
import functools

import jax
import jax.numpy as jnp
from jax import lax
from jax.experimental import pallas as pl
from jax.experimental.pallas import tpu as pltpu
from jax.sharding import PartitionSpec as P

CH_SUB = 128
SUBT = 2
SPAN = 8
KMAX = 8
LANES = 128
PER_LAG = CH_SUB // KMAX
VMEM = pltpu.MemorySpace.VMEM
SMEM = pltpu.MemorySpace.SMEM
IN_VMEM = pl.BlockSpec(memory_space=VMEM)
IN_SMEM = pl.BlockSpec(memory_space=SMEM)


def in_vmem(x):
    return pltpu.with_memory_space_constraint(x, VMEM)


def in_smem(x):
    return pltpu.with_memory_space_constraint(x, SMEM)


def cost(flops, read):
    return pl.CostEstimate(flops=flops, bytes_accessed=read, transcendentals=0)


def swap(x, bit, group):
    return lax.ppermute(x, "trials", [(i, i ^ bit) for i in range(group)])


def shifted(x, k):
    lane = lax.broadcasted_iota(jnp.int32, x.shape, 1)
    row = lax.broadcasted_iota(jnp.int32, x.shape, 0)
    here = pltpu.roll(x, LANES - k, 1)
    after = pltpu.roll(here, x.shape[0] - 1, 0)
    after = jnp.where(row == x.shape[0] - 1, 0.0, after)
    return jnp.where(lane < LANES - k, here, after)


def raw_kernel(chunks, x_hbm, delays_hbm, out, rows, x, delays, sems):
    blocks = x.shape[1] // LANES
    width = x.shape[1] // chunks
    copies = []
    for i in range(chunks):
        part = pl.ds(i * width, width)
        copies.append(pltpu.make_async_copy(x_hbm.at[:, part], x.at[:, part], sems.at[i]))
        copies[-1].start()
    copies.append(pltpu.make_async_copy(delays_hbm, delays, sems.at[chunks]))
    copies[-1].start()
    row = lax.broadcasted_iota(jnp.int32, (2 * KMAX, CH_SUB), 0)
    chan = lax.broadcasted_iota(jnp.int32, (2 * KMAX, CH_SUB), 1)
    select = ((row >= KMAX) | (chan // PER_LAG == KMAX - 1 - row)).astype(jnp.bfloat16)
    sub = lax.broadcasted_iota(jnp.int32, (KMAX, LANES), 0)
    lane = lax.broadcasted_iota(jnp.int32, (KMAX, LANES), 1)
    stays = lane < LANES - (KMAX - 1 - sub)
    rows[...] = jnp.zeros_like(rows)
    rolled, plain = [], []

    def finish(b0):
        first = plain[b0]
        for k in range(1, 8):
            first = jnp.where(sub == k, plain[b0 + k], first)
        out[0, b0 : b0 + 8] = first
        level = [jnp.where(stays, rolled[b], rolled[b + 1]) for b in range(b0, b0 + 8)]
        for half in (4, 2, 1):
            low = (sub & half) == 0
            level = [
                jnp.where(low, level[k] + pltpu.roll(level[k], 8 - half, 0), level[k + half] + pltpu.roll(level[k + half], half, 0))
                for k in range(half)
            ]
        out[1, b0 : b0 + 8] = level[0]

    for b0 in range(0, blocks, 8):
        if b0 * LANES % width == 0:
            copies[b0 * LANES // width].wait()
        part = x[:, b0 * LANES : (b0 + 8) * LANES]
        sums = jnp.dot(select, part, preferred_element_type=jnp.float32)
        for b in range(8):
            cut = sums[:KMAX, b * LANES : (b + 1) * LANES]
            rolled.append(pltpu.roll(cut, LANES - (KMAX - 1), 1, stride=1, stride_axis=0))
            plain.append(sums[KMAX:, b * LANES : (b + 1) * LANES])
        if b0:
            finish(b0 - 8)
    rolled.append(jnp.zeros((KMAX, LANES), jnp.float32))
    finish(blocks - 8)
    copies[chunks].wait()
    rows[: delays.shape[0], : delays.shape[1]] = delays[...]


def raw_series(spectra, delays):
    channels, samples = spectra.shape
    chunks = 2
    return pl.pallas_call(
        functools.partial(raw_kernel, chunks),
        out_shape=(VMEM((SUBT, samples // LANES, LANES), jnp.float32), VMEM((8, LANES), jnp.int32)),
        in_specs=[pl.BlockSpec(memory_space=pl.ANY)] * 2,
        out_specs=(IN_VMEM,) * 2,
        scratch_shapes=[
            pltpu.VMEM(spectra.shape, spectra.dtype),
            pltpu.VMEM(delays.shape, delays.dtype),
            pltpu.SemaphoreType.DMA((chunks + 1,)),
        ],
        cost_estimate=cost(4 * KMAX * channels * samples, 2 * channels * samples),
    )(spectra, delays)


def scalars_kernel(trials, group, x, out):
    if x.shape[0] * group <= 16:
        for e in range(x.shape[0]):
            tile = x[e]
            for i in range(trials):
                for s in range(group):
                    out[e, i, s] = tile[i, s]
    else:
        pltpu.sync_copy(x, out)


def to_scalars(x, trials, group, estimate):
    return pl.pallas_call(
        functools.partial(scalars_kernel, trials, group),
        out_shape=SMEM(x.shape, x.dtype),
        in_specs=[IN_VMEM],
        out_specs=IN_SMEM,
        cost_estimate=estimate,
    )(in_vmem(x))


def tables_kernel(channels, widths, spans, bands, scale, mask):
    lag = lax.broadcasted_iota(jnp.int32, (LANES, LANES), 1) - lax.broadcasted_iota(jnp.int32, (LANES, LANES), 0)
    row = lax.broadcasted_iota(jnp.int32, (SPAN, LANES), 0)
    for n in range(widths.shape[0]):
        width = widths[n]
        cols = pl.ds(n * LANES, LANES)
        bands[:LANES, cols] = ((lag >= 0) & (lag < width)).astype(jnp.bfloat16)
        bands[LANES:, cols] = (lag + LANES < width).astype(jnp.bfloat16)
        scale[n : n + 1] = 1.0 / (jnp.sqrt(jnp.full((1, LANES), width, jnp.float32)) * (channels**0.5))
    mask[...] = (row < spans[lax.axis_index("trials")]).astype(jnp.float32)


def tables(widths, spans, channels):
    nw = widths.shape[0]
    return pl.pallas_call(
        functools.partial(tables_kernel, channels),
        out_shape=(
            VMEM((2 * LANES, nw * LANES), jnp.bfloat16),
            VMEM((nw, LANES), jnp.float32),
            VMEM((SPAN, LANES), jnp.float32),
        ),
        in_specs=[IN_SMEM] * 2,
        out_specs=(IN_VMEM,) * 3,
        cost_estimate=cost(0, 1 << 20),
    )(widths, spans)


def windows(out, raw, masks, mean, delays, e, trials, group):
    me = lax.axis_index("trials")
    for i in range(trials):
        j = i % SUBT
        acc = None
        for a, ref in enumerate(raw):
            cut = ref[j, pl.ds(delays[e, i, me ^ masks[a]], SPAN), :]
            acc = cut if acc is None else acc + cut
        less = None
        if group <= 16:
            for s in range(group):
                cut = mean[j, pl.ds(delays[e, i, s], SPAN), :]
                less = cut if less is None else less + cut
        else:
            less = lax.fori_loop(
                0, group, lambda s, v: v + mean[j, pl.ds(delays[e, i, s], SPAN), :], jnp.zeros_like(acc)
            )
        out[i] = acc - less


def far_kernel(masks, trials, group, channels, *refs):
    known = len(masks)
    raw, (far, out, mean) = refs[:known], refs[known:]
    total = raw[0][0]
    for a in range(1, known):
        total = total + raw[a][0]
    mean[0] = total * (CH_SUB / channels)
    total = total * (PER_LAG / channels)
    for k in (1, 2, 4):
        total = total + shifted(total, k)
    mean[1] = total

    def one(e):
        windows(out.at[e], raw, masks, mean, far, e, trials, group)

    if out.shape[0] == 1:
        one(0)
    else:
        pl.loop(0, out.shape[0])(one)


def far_sums(raw, masks, far, trials, group):
    return pl.pallas_call(
        functools.partial(far_kernel, masks, trials, group, CH_SUB * group),
        out_shape=(VMEM((far.shape[0], trials, SPAN, LANES), jnp.float32), VMEM(raw[0].shape, jnp.float32)),
        in_specs=[IN_VMEM] * len(raw) + [IN_SMEM],
        out_specs=(IN_VMEM,) * 2,
        cost_estimate=cost(0, 1 << 20),
    )(*[in_vmem(v) for v in raw], in_smem(far))


def near_kernel(masks, trials, group, *refs):
    known = len(masks)
    raw, (mean, near, out) = refs[:known], refs[known:]
    windows(out, raw, masks, mean, near, 0, trials, group)


def near_sums(raw, masks, mean, near, trials, group):
    return pl.pallas_call(
        functools.partial(near_kernel, masks, trials, group),
        out_shape=VMEM((trials, SPAN, LANES), jnp.float32),
        in_specs=[IN_VMEM] * (len(raw) + 1) + [IN_SMEM],
        out_specs=IN_VMEM,
        cost_estimate=cost(0, 1 << 20),
    )(*[in_vmem(v) for v in (*raw, mean)], in_smem(near))


def boxcar_kernel(a, b, bands, scale, mask, out, y, sems):
    trials = a.shape[0]
    rows = trials * SPAN
    trial = jnp.where(mask[...][None] > 0.0, a[...] + b[...], 0.0).reshape(rows, LANES)
    block = lax.broadcasted_iota(jnp.int32, trial.shape, 0) % SPAN
    before = jnp.where(block >= 1, pltpu.roll(trial, 1, 0), 0.0)
    rest = jnp.concatenate([trial, before], axis=1)
    pieces = []
    for _ in range(3):
        pieces.append(rest.astype(jnp.bfloat16))
        rest = rest - pieces[-1].astype(jnp.float32)
    sums = jnp.dot(jnp.concatenate(pieces, axis=0), bands[...], preferred_element_type=jnp.float32)
    sums = sums[:rows] + (sums[rows : 2 * rows] + sums[2 * rows :])
    copies = []
    for t in range(trials):
        for n in range(scale.shape[0]):
            y[t, :, n, :] = sums[t * SPAN : (t + 1) * SPAN, n * LANES : (n + 1) * LANES] * scale[n : n + 1]
        copies.append(pltpu.make_async_copy(y.at[t], out.at[t], sems.at[t]))
        copies[-1].start()
    for c in copies:
        c.wait()


def boxcars(a, b, bands, scale, mask):
    trials, nw = a.shape[0], scale.shape[0]
    shape = (trials, SPAN, nw, LANES)
    out = pl.pallas_call(
        boxcar_kernel,
        out_shape=jax.ShapeDtypeStruct(shape, jnp.float32),
        in_specs=[IN_VMEM] * 5,
        out_specs=pl.BlockSpec(memory_space=pl.ANY),
        scratch_shapes=[pltpu.VMEM(shape, jnp.float32), pltpu.SemaphoreType.DMA((trials,))],
        cost_estimate=cost(0, 1 << 20),
    )(*[in_vmem(v) for v in (a, b, bands, scale, mask)])
    return out.transpose(0, 2, 1, 3).reshape(trials, nw, SPAN * LANES)


def on_device(spectra, delays, spans, widths):
    group = lax.axis_size("trials")
    channels = CH_SUB * group
    trials = delays.shape[0]
    far_bits = [b for b in (9, 16, 32, 64, 128, 256) if b < group]

    raw, rows = raw_series(spectra, delays)
    masks = (0, 2, 4, 7)
    raws = [raw] + [swap(raw, m, group) for m in masks[1:]]
    raws = raws + [swap(r, 1, group) for r in raws]
    masks = masks + tuple(m ^ 1 for m in masks)
    owned = rows[None]
    for b in far_bits:
        owned = jnp.concatenate([owned, swap(owned, b, group)])
    boxes = tables(widths, spans, channels)

    near = to_scalars(rows[None], trials, group, cost(0, 1 << 20))
    away = to_scalars(owned[1:], trials, group, cost(1 << 34, 1 << 24))
    far, mean = far_sums(raws, masks, away, trials, group)
    sums = jnp.concatenate([near_sums(raws, masks, mean, near, trials, group)[None], far])
    for b in reversed(far_bits):
        half = sums.shape[0] // 2
        mine, theirs = sums[:half], swap(sums[half:], b, group)
        sums = mine + theirs
    return boxcars(mine[0], theirs[0], *boxes)


def solution(mesh):
    in_specs = (P(("beams", "trials"), None), P("trials", None), P(), P())
    out_specs = P(("beams", "trials"), None, None)
    return jax.shard_map(
        on_device, mesh=mesh, in_specs=in_specs, out_specs=out_specs, check_vma=False
    )
```
